128 devices in a mesh: row: 16 (over x, y), col: 8 (over z, core).
Axes of the slice: x: 4, y: 4, z: 4, core: 2. Of those that a mesh axis runs over, the one named last changes fastest.
Arguments:
- tiles: bfloat16 [65536, 128, 128], P(('row', 'col'))
- row_tiles: int32 [65536], P(('row', 'col')), may hold values from 0 to 255, as said below
- col_tiles: int32 [65536], P(('row', 'col')), may hold values from 0 to 4095, as said below
- counts: int32 [128], P(('row', 'col')), may hold values from 128 to 512, as said below
- right_basis: float32 [100, 524288], P(None, ('row', 'col'))
- left_basis: float32 [100, 524288], P(None, ('row', 'col'))
- start: float32 [524288], P(('row', 'col'))
Outputs:
- left_vectors: float32 [2, 524288], P(None, ('row', 'col'))
- right_vectors: float32 [2, 524288], P(None, ('row', 'col'))
- coefficients: float32 [5], replicated
The draws below stay inside these ranges and needn't reach their ends.
Inputs may be any that keep to these rules, and one draw needn't show every extreme that they name: `row_tiles`: tile rows lie within a row group. `col_tiles`: device d owns tile columns d * 32 up to (d + 1) * 32 - 1. The 512 slots of one device name at most 8 distinct tile columns owned by any one device; in every draw some owner receives exactly 8 distinct live tile columns from every device. `counts`: slots at or beyond a block's count hold no part of the matrix; in every draw some block has 512 live slots.
All inputs are finite; a program needn't handle non-finite values.
Results may differ from the reference program's by a relative error of at most 0.0045.
The reference program's roundings to bfloat16 on the way count: a program that leaves them out, or rounds other values in their place, can miss the bound.
Values may be sent and summed in bfloat16 or wider, within the bound.
No kernel may reach another device: no remote copies, remote signals or barrier semaphores. Data moves between devices by JAX's collectives and lax.ppermute only.
A program may use at most 128 MiB of HBM per device.

```python
import jax
import jax.numpy as jnp
from jax import lax

ROWS_DEV = 4096
TPD = 512
TILE = 128
K = 100
PEER_TILES = 8
ROWS = 524288
NTILES = 4096
GROUP_TILES = 256
TILES_ALL = 65536
N_ROW = 16
N_COL = 8


def layout(key):
    base = jax.random.fold_in(key, 11)
    devices = TILES_ALL // TPD
    per_owner = ROWS_DEV // TILE
    first_ids = jax.random.randint(jax.random.fold_in(base, 1), (TILES_ALL,), 0, GROUP_TILES)
    second_ids = jax.random.randint(jax.random.fold_in(base, 2), (TILES_ALL,), 0, GROUP_TILES)
    row_ids = jnp.minimum(first_ids, second_ids).astype(jnp.int32)
    owners = jax.random.randint(jax.random.fold_in(base, 3), (TILES_ALL,), 0, devices)
    picks = jax.random.randint(jax.random.fold_in(base, 4), (TILES_ALL,), 0, PEER_TILES)
    scores = jax.random.randint(jax.random.fold_in(base, 5), (devices, devices, per_owner), 0, 1048576) * per_owner + jnp.arange(per_owner, dtype=jnp.int32)
    ranked = jnp.argsort(scores, axis=-1)[:, :, :PEER_TILES].astype(jnp.int32)
    special_owner = jax.random.randint(jax.random.fold_in(base, 6), (), 0, devices)
    slot_place = jnp.arange(TILES_ALL, dtype=jnp.int32) % TPD
    leading = slot_place < PEER_TILES
    owners = jnp.where(leading, special_owner, owners)
    picks = jnp.where(leading, slot_place, picks)
    sender = jnp.arange(TILES_ALL, dtype=jnp.int32) // TPD
    col_ids = (owners * per_owner + ranked[sender, owners, picks]).astype(jnp.int32)
    levels = jax.random.randint(jax.random.fold_in(base, 7), (devices,), 0, 8)
    counts = jnp.where(levels < 3, TPD, jnp.where(levels < 6, TPD // 2, TPD // 4))
    chosen = jax.random.randint(jax.random.fold_in(base, 8), (), 0, devices)
    counts = jnp.where(jnp.arange(devices) == chosen, TPD, counts).astype(jnp.int32)
    return (row_ids, col_ids, counts)


def tile_values(key):
    return jax.random.normal(jax.random.fold_in(key, 12), (TILES_ALL, TILE, TILE), jnp.float32) * (0.35 / TILE ** 0.5)


def noises(key):
    first_key = jax.random.fold_in(key, 14)
    second_key = jax.random.fold_in(key, 15)
    return (jax.random.normal(first_key, (ROWS,), jnp.float32), jax.random.normal(second_key, (ROWS,), jnp.float32))


def right_values(key):
    own_part = jax.random.normal(jax.random.fold_in(key, 13), (K, ROWS), jnp.float32)
    shared_part = jax.random.normal(jax.random.fold_in(key, 18), (ROWS,), jnp.float32)
    return own_part + 0.1 * shared_part[None, :]


def apply_rows(key, vector):
    devices = TILES_ALL // TPD
    col_count = GROUP_TILES * TILE // ROWS_DEV
    row_ids, col_ids, counts = layout(key)
    table = vector.reshape(NTILES, TILE)
    slots = jnp.arange(TPD)
    members = (tile_values(key).reshape(devices, TPD, TILE, TILE), row_ids.reshape(devices, TPD), col_ids.reshape(devices, TPD), counts, jnp.arange(devices))

    def advance(running, member):
        blocks, rows_here, cols_here, count, device = member
        weights = (slots < count).astype(jnp.float32)
        products = jnp.einsum('tij,tj->ti', blocks, table[cols_here]) * weights[:, None]
        target = device // col_count * GROUP_TILES + rows_here
        return (running + jax.ops.segment_sum(products, target, num_segments=NTILES), None)
    return lax.scan(advance, jnp.zeros((NTILES, TILE), jnp.float32), members)[0].reshape(-1)


def draw_tiles(key, part):
    return tile_values(key).astype(jnp.bfloat16)


def draw_row_tiles(key, part):
    return layout(key)[0]


def draw_col_tiles(key, part):
    return layout(key)[1]


def draw_counts(key, part):
    return layout(key)[2]


def draw_right_basis(key, part):
    return right_values(key)


def draw_left_basis(key, part):
    first_noise = noises(key)[0]
    image = apply_rows(key, first_noise)
    image = image / jnp.sqrt(jnp.mean(image * image) + 1e-06)
    own_part = jax.random.normal(jax.random.fold_in(key, 16), (K, ROWS), jnp.float32)
    shared_part = jax.random.normal(jax.random.fold_in(key, 19), (ROWS,), jnp.float32)
    others = own_part + 0.1 * shared_part[None, :]
    return others.at[0].set(image)


def draw_start(key, part):
    first_noise, second_noise = noises(key)
    raw_mix = jax.random.normal(jax.random.fold_in(key, 17), (K,), jnp.float32)
    mixing = (raw_mix - jnp.mean(raw_mix)) * (1.2 / K ** 0.5) + 2.5 / K
    return first_noise + second_noise + jnp.dot(mixing, right_values(key))


def setup_inputs(seed: int = 0) -> dict:
    key_list = jax.random.split(jax.random.key(seed), 8)
    return {
        "tiles": draw_tiles(jax.random.fold_in(key_list[7], 71), 0),
        "row_tiles": draw_row_tiles(jax.random.fold_in(key_list[7], 71), 0),
        "col_tiles": draw_col_tiles(jax.random.fold_in(key_list[7], 71), 0),
        "counts": draw_counts(jax.random.fold_in(key_list[7], 71), 0),
        "right_basis": draw_right_basis(jax.random.fold_in(key_list[7], 71), 0),
        "left_basis": draw_left_basis(jax.random.fold_in(key_list[7], 71), 0),
        "start": draw_start(jax.random.fold_in(key_list[7], 71), 0),
    }


HIGH = lax.Precision.HIGHEST

def sparse_rows(tiles, row_tiles, col_tiles, counts, vector):
    devices = N_ROW * N_COL
    table = vector.astype(jnp.float32).reshape(NTILES, TILE)
    slots = jnp.arange(TPD, dtype=jnp.int32)
    members = (tiles.reshape(devices, TPD, TILE, TILE), row_tiles.reshape(devices, TPD), col_tiles.reshape(devices, TPD), counts, jnp.arange(devices, dtype=jnp.int32))

    def advance(running, member):
        blocks, rows_here, cols_here, count, device = member
        weights = (slots < count).astype(jnp.float32)
        products = jnp.einsum('tij,tj->ti', blocks.astype(jnp.float32), table[cols_here], precision=HIGH) * weights[:, None]
        target = (device // N_COL * GROUP_TILES + rows_here).astype(jnp.int32)
        return (running + jax.ops.segment_sum(products, target, num_segments=NTILES), None)
    summed = lax.scan(advance, jnp.zeros((NTILES, TILE), jnp.float32), members)[0]
    return summed.reshape(-1)

def sparse_columns(tiles, row_tiles, col_tiles, counts, vector):
    devices = N_ROW * N_COL
    table = vector.astype(jnp.float32).reshape(NTILES, TILE)
    slots = jnp.arange(TPD, dtype=jnp.int32)
    members = (tiles.reshape(devices, TPD, TILE, TILE), row_tiles.reshape(devices, TPD), col_tiles.reshape(devices, TPD), counts, jnp.arange(devices, dtype=jnp.int32))

    def advance(running, member):
        blocks, rows_here, cols_here, count, device = member
        weights = (slots < count).astype(jnp.float32)
        source = (device // N_COL * GROUP_TILES + rows_here).astype(jnp.int32)
        products = jnp.einsum('tij,ti->tj', blocks.astype(jnp.float32), table[source], precision=HIGH) * weights[:, None]
        return (running + jax.ops.segment_sum(products, cols_here, num_segments=NTILES), None)
    summed = lax.scan(advance, jnp.zeros((NTILES, TILE), jnp.float32), members)[0]
    return summed.reshape(-1)

def orthogonalize(vector, basis):
    coeffs = jnp.dot(basis, vector, precision=HIGH) / ROWS
    remainder = vector - jnp.dot(coeffs, basis, precision=HIGH)
    norm_value = jnp.sqrt(jnp.sum(remainder * remainder) / ROWS + 1e-06)
    return (remainder / norm_value, norm_value)

def reference(tiles, row_tiles, col_tiles, counts, right_basis, left_basis, start):
    right_one, beta_zero = orthogonalize(start, right_basis)
    image = sparse_rows(tiles, row_tiles, col_tiles, counts, right_one.astype(jnp.bfloat16))
    left_one, alpha_one = orthogonalize(image, left_basis)
    back = sparse_columns(tiles, row_tiles, col_tiles, counts, left_one.astype(jnp.bfloat16)) - alpha_one * right_one
    right_two, beta_one = orthogonalize(back, right_basis)
    image = sparse_rows(tiles, row_tiles, col_tiles, counts, right_two.astype(jnp.bfloat16)) - beta_one * left_one
    left_two, alpha_two = orthogonalize(image, left_basis)
    back = sparse_columns(tiles, row_tiles, col_tiles, counts, left_two.astype(jnp.bfloat16)) - alpha_two * right_two
    right_three, beta_two = orthogonalize(back, right_basis)
    return (jnp.stack([left_one, left_two]), jnp.stack([right_two, right_three]), jnp.stack([beta_zero, alpha_one, beta_one, alpha_two, beta_two]))
```

```python
import functools

import jax
import jax.numpy as jnp
from jax import lax
from jax.experimental import pallas as pl
from jax.experimental.pallas import tpu as pltpu
from jax.sharding import Mesh
from jax.sharding import PartitionSpec as P

PEER_TILES = 8
COL = ("col_0", "col_1")
ALL = ("row_0", "row_1", "col_0", "col_1")
HIGH = lax.Precision.HIGHEST
F32, BF16, I32 = jnp.float32, jnp.bfloat16, jnp.int32

DEV = 128
OWN = 32
TILE = 128
SLOTS = 512
GROUP = 256
NAMED = DEV * PEER_TILES
PLACE = 104
EXTRA = PEER_TILES + 3


def iota(shape, dim):
    return lax.broadcasted_iota(I32, shape, dim)


def one_hot(condition):
    return jnp.where(condition, 1.0, 0.0).astype(BF16)


def dot(a, b, ca=1, cb=0, precision=None):
    return lax.dot_general(
        a, b, (((ca,), (cb,)), ((), ())), precision=precision, preferred_element_type=F32
    )


def selected(hot, value):
    first = value.astype(BF16)
    rest = value - first.astype(F32)
    second = rest.astype(BF16)
    third = (rest - second.astype(F32)).astype(BF16)
    return dot(hot, third) + dot(hot, second) + dot(hot, first)


def products_row(basis, vector, held):
    size = basis.shape[0]
    total = basis[:, 0:TILE] * vector[0:1, :]
    for k in range(1, OWN):
        total = total + basis[:, k * TILE : (k + 1) * TILE] * vector[k : k + 1, :]
    held[...] = jnp.zeros_like(held)
    held[0:size, :] = total
    row = dot(jnp.ones((8, TILE), F32), held[...], 1, 1, HIGH)[0:1, :]
    square = jnp.sum(vector * vector, keepdims=True)
    return jnp.where(iota((1, TILE), 1) == size, square, row)


def coefficients_of(total, size, row_total):
    lane = iota((1, TILE), 1)
    projection = jnp.where(lane < size, total, 0.0)
    square = jnp.sum(jnp.where(lane == size, total, 0.0), axis=1, keepdims=True)
    coeffs = projection / row_total
    diagonal = iota((size, TILE), 0) == iota((size, TILE), 1)
    column = jnp.sum(jnp.where(diagonal, coeffs, 0.0), axis=1, keepdims=True)
    return projection, square, coeffs, column


def subtract_basis(out, vector, basis, column):
    wide = jnp.broadcast_to(column, (column.shape[0], TILE))
    for k in range(OWN):
        part = jnp.sum(basis[:, k * TILE : (k + 1) * TILE] * wide, axis=0, keepdims=True)
        out[k : k + 1, :] = vector[k : k + 1, :] - part


def norm_of(projection, square, coeffs, column, gram, row_total):
    size = column.shape[0]
    applied = jnp.sum(gram[0:size, :] * coeffs, axis=1, keepdims=True)
    quadratic = jnp.sum(applied * column, axis=0, keepdims=True)
    linear = jnp.sum(coeffs * projection, axis=1, keepdims=True)
    left = jnp.maximum(square - 2.0 * linear + quadratic, 0.0)
    return jnp.sqrt(left / row_total + 1e-06)


def first_sums(col_row, basis, start, out, held):
    owner, place = col_row[...] // OWN, col_row[...] % OWN
    owners = one_hot(iota((DEV, SLOTS), 0) == owner)
    places = one_hot(iota((OWN, SLOTS), 0) == place)
    touched = dot(places, owners, 1, 1) > 0.5
    below = one_hot(iota((OWN, OWN), 1) < iota((OWN, OWN), 0))
    rank = dot(below, one_hot(touched))
    row = products_row(basis, start[...], held)
    held[...] = jnp.zeros_like(held)
    number = (iota((OWN, DEV), 0) + 1).astype(F32)
    for k in range(PEER_TILES):
        here = touched & (rank > k - 0.5) & (rank < k + 0.5)
        named = jnp.sum(jnp.where(here, number, 0.0), axis=0, keepdims=True)
        held[PLACE + k : PLACE + k + 1, :] = named - 1.0
    out[:, 0, :] = held[...].T + row


def tables(counts, col_row, col_col, right, left, pos_row, pos_col, gram_r, gram_l):
    count = counts[0]
    owner, place = col_row[...] // OWN, col_row[...] % OWN
    owners = one_hot(iota((DEV, SLOTS), 0) == owner)
    in_place = iota((OWN, SLOTS), 0) == place
    touched = one_hot(dot(one_hot(in_place), owners, 1, 1) > 0.5)
    below = one_hot(iota((OWN, OWN), 1) < iota((OWN, OWN), 0))
    rank = dot(below, touched).astype(BF16)
    mine = dot(rank, owners)
    mine = jnp.sum(jnp.where(in_place, mine, 0.0), axis=0, keepdims=True)
    position = owner * PEER_TILES + mine.astype(I32)
    pos_row[...] = jnp.where(iota((1, SLOTS), 1) < count, position, -1)
    owner, place = col_col[...] // OWN, col_col[...] % OWN
    owners = one_hot(iota((SLOTS, DEV), 1) == owner)
    mine = dot(owners, rank, 1, 1)
    mine = jnp.where(iota((SLOTS, OWN), 1) == place, mine, 0.0)
    position = owner * PEER_TILES + jnp.sum(mine, axis=1, keepdims=True).astype(I32)
    pos_col[...] = jnp.where(iota((SLOTS, 1), 0) < count, position, -1)
    for basis, gram in ((right, gram_r), (left, gram_l)):
        size = basis.shape[0]
        gram[...] = jnp.zeros_like(gram)
        gram[0:size, 0:size] = dot(basis[...], basis[...], 1, 1, HIGH)


def place_row_of(arrived):
    lane = iota((DEV, NAMED), 0)
    spread = dot(arrived.astype(BF16), one_hot(lane - PLACE == iota((DEV, NAMED), 1) % PEER_TILES))
    own = iota((DEV, NAMED), 1) // PEER_TILES == lane
    row = jnp.sum(jnp.where(own, spread, 0.0), axis=0, keepdims=True)
    return jnp.round(row).astype(I32)


def first_vector(row_total, arrived, start, basis, gram_r, gram_l, rest, send, place_row):
    size = basis.shape[0]
    got = arrived[:, 0, :]
    total = jnp.sum(got, axis=0, keepdims=True)
    _, _, _, column = coefficients_of(total, size, row_total)
    subtract_basis(rest, start, basis, column)
    vector = rest[...]
    named = place_row_of(got)
    place_row[...] = named
    hot = jnp.where(iota((OWN, NAMED), 0) == named, 1.0, 0.0)
    blocks = dot(hot, vector, 0, 0, HIGH).reshape(DEV, PEER_TILES, TILE)
    for k in range(PEER_TILES):
        send[:, k, 0, :] = blocks[:, k, :]
    square = jnp.sum(vector * vector, keepdims=True)
    send[:, PEER_TILES, 0, :] = jnp.broadcast_to(square, (DEV, TILE))
    send[:, PEER_TILES + 1, 0, :] = gram_r[...]
    send[:, PEER_TILES + 2, 0, :] = gram_l[...]


def tiles_times(sources, tiles, products):
    many = 16

    def step(i, carry):
        at = pl.multiple_of(i * many, many)
        block = tiles[pl.ds(at, many)].reshape(many * TILE, TILE)
        wide = dot(sources[pl.ds(at, many), :], block, 1, 1)
        row = iota((many, TILE), 0)
        total = jnp.where(row == 0, wide[:, 0:TILE], 0.0)
        for j in range(1, many):
            total = jnp.where(row == j, wide[:, j * TILE : (j + 1) * TILE], total)
        products[pl.ds(at, many), :] = total
        return carry

    lax.fori_loop(0, SLOTS // many, step, 0, unroll=4)


def times_tiles(sources, tiles, products):
    many = 16

    def step(i, carry):
        at = pl.multiple_of(i * many, many)
        block = tiles[pl.ds(at, many)].reshape(many * TILE, TILE)
        mine = sources[pl.ds(at, many), :]
        row = iota((many, TILE), 0)
        parts = [jnp.where(row == j, mine, jnp.zeros_like(mine)) for j in range(many)]
        products[pl.ds(at, many), :] = dot(jnp.concatenate(parts, axis=1), block)
        return carry

    lax.fori_loop(0, SLOTS // many, step, 0, unroll=4)


def summed_by_row(row_row, products, out):
    rows = one_hot(iota((GROUP, SLOTS), 0) == row_row[...])
    out[...] = selected(rows, products[...]).reshape(out.shape)


def rows_product_first(
    row_total, arrived, pos_col, row_row, tiles, out, norm, grams, sources, products
):
    total = jnp.sum(arrived[:, PEER_TILES, 0, :], axis=0, keepdims=True)
    size = jnp.sqrt(total / row_total + 1e-06)
    norm[...] = size
    grams[0:1, :] = jnp.sum(arrived[:, PEER_TILES + 1, 0, :], axis=0, keepdims=True)
    grams[1:2, :] = jnp.sum(arrived[:, PEER_TILES + 2, 0, :], axis=0, keepdims=True)
    values = jnp.zeros((SLOTS, TILE), F32)
    for k in range(PEER_TILES):
        vector = (arrived[:, k, 0, :] / size).astype(BF16)
        hot = one_hot(iota((SLOTS, DEV), 1) * PEER_TILES + k == pos_col[...])
        values = values + dot(hot, vector)
    sources[...] = values.astype(BF16)
    tiles_times(sources, tiles, products)
    summed_by_row(row_row, products, out)


def rows_product(arrived, pos_col, row_row, tiles, out, sources, products):
    hot = one_hot(iota((SLOTS, NAMED), 1) == pos_col[...])
    vector = arrived[...].reshape(NAMED, TILE)
    sources[...] = dot(hot, vector).astype(BF16)
    tiles_times(sources, tiles, products)
    summed_by_row(row_row, products, out)


def column_product(arrived, row_col, pos_row, tiles, out, sources, products):
    hot = one_hot(iota((SLOTS, GROUP), 1) == row_col[...])
    vector = arrived[...].reshape(GROUP, TILE)
    sources[...] = dot(hot, vector).astype(BF16)
    times_tiles(sources, tiles, products)
    hot = one_hot(iota((NAMED, SLOTS), 0) == pos_row[...])
    out[...] = selected(hot, products[...]).reshape(out.shape)


def image_sums_first(arrived, basis, grams, image, out, held):
    vector = jnp.sum(arrived[...], axis=0)
    image[...] = vector
    row = products_row(basis, vector, held)
    out[:, 0, 0:TILE] = jnp.broadcast_to(row, (DEV, TILE))
    out[:, 0, TILE : 2 * TILE] = jnp.broadcast_to(grams[0:1, :], (DEV, TILE))
    out[:, 0, 2 * TILE : 3 * TILE] = jnp.broadcast_to(grams[1:2, :], (DEV, TILE))


def image_sums(arrived, basis, earlier, factor, image, out, held):
    vector = jnp.sum(arrived[...], axis=0) - factor[...] * earlier[...]
    image[...] = vector
    out[:, 0, :] = jnp.broadcast_to(products_row(basis, vector, held), (DEV, TILE))


def back_sums(divide, arrived, basis, place_row, earlier, by, factor, back, out, held):
    hot = one_hot(iota((OWN, NAMED), 0) == place_row[...])
    before = earlier[...] / by[...] if divide else earlier[...]
    vector = selected(hot, arrived[...].reshape(NAMED, TILE)) - factor[...] * before
    back[...] = vector
    out[:, 0, :] = jnp.broadcast_to(products_row(basis, vector, held), (DEV, TILE))


def left_vector_first(row_total, arrived, image, basis, new, copies, norm, gram_r, gram_l):
    got = arrived[:, 0, :]
    gram_r[...] = got[:, TILE : 2 * TILE]
    gram_l[...] = got[:, 2 * TILE : 3 * TILE]
    total = jnp.sum(got[:, 0:TILE], axis=0, keepdims=True)
    finish(row_total, total, image, basis, gram_l, new, norm)
    copies[...] = jnp.broadcast_to(new[...].astype(BF16), copies.shape)


def finish(row_total, total, vector, basis, gram, new, norm):
    size = basis.shape[0]
    projection, square, coeffs, column = coefficients_of(total, size, row_total)
    factor = norm_of(projection, square, coeffs, column, gram, row_total)
    norm[...] = jnp.broadcast_to(factor, (1, TILE))
    subtract_basis(new, vector, basis, column)
    new[...] = new[...] / factor


def lines(out, at, vector):
    for k in range(OWN):
        out[at : at + 1, k * TILE : (k + 1) * TILE] = vector[k : k + 1, :]


def left_vector(row_total, arrived, image, basis, gram, earlier, new_pair, copies, norm, new):
    total = jnp.sum(arrived[:, 0, :], axis=0, keepdims=True)
    finish(row_total, total, image, basis, gram, new, norm)
    copies[...] = jnp.broadcast_to(new[...].astype(BF16), copies.shape)
    lines(new_pair, 0, earlier)
    lines(new_pair, 1, new)


def right_vector(row_total, arrived, back, basis, gram, place_row, new, send, norm):
    total = jnp.sum(arrived[:, 0, :], axis=0, keepdims=True)
    finish(row_total, total, back, basis, gram, new, norm)
    hot = one_hot(iota((OWN, NAMED), 0) == place_row[...])
    blocks = dot(hot, new[...].astype(BF16), 0, 0)
    send[...] = blocks.astype(BF16).reshape(send.shape)


def last_vector(row_total, arrived, back, basis, gram, earlier, *rest):
    norms, (new_pair, factors, new, norm) = rest[:4], rest[4:]
    total = jnp.sum(arrived[:, 0, :], axis=0, keepdims=True)
    finish(row_total, total, back, basis, gram, new, norm)
    lines(new_pair, 0, earlier)
    lines(new_pair, 1, new)
    for i, value in enumerate((*norms, norm)):
        factors[i] = jnp.max(value[...])


VMEM = pl.BlockSpec(memory_space=pltpu.VMEM)
SMEM = pl.BlockSpec(memory_space=pltpu.SMEM)


def call(body, outs, args, scratch=(), in_specs=None, out_specs=None, mib=24):
    shapes = [jax.ShapeDtypeStruct(s, d) for s, d in outs]
    return pl.pallas_call(
        body,
        out_shape=shapes,
        in_specs=in_specs or [VMEM] * len(args),
        out_specs=out_specs or [VMEM] * len(outs),
        scratch_shapes=[pltpu.VMEM(s, d) for s, d in scratch],
        compiler_params=pltpu.CompilerParams(vmem_limit_bytes=mib << 20),
    )(*args)


def to_all(value):
    return lax.all_to_all(value, ALL, 0, 0, tiled=True)


def in_group(value):
    return lax.all_to_all(value, COL, 0, 0, tiled=True)


def shards(tiles, row_tiles, col_tiles, counts, right_basis, left_basis, start):
    row_total = float(start.shape[0] * DEV)
    with_total = lambda body: functools.partial(body, row_total)
    own = ((OWN, TILE), F32)
    line = ((1, TILE), F32)
    square = ((DEV, TILE), F32)
    sums = ((DEV, 1, TILE), F32)
    blocks = (DEV, PEER_TILES, TILE)
    in_rows = ((8, OWN, TILE), F32)
    copied = ((8, OWN, TILE), BF16)
    work = [((SLOTS, TILE), BF16), ((SLOTS, TILE), F32)]
    right, left = right_basis, left_basis
    begin = start.reshape(OWN, TILE)
    col_row, col_col = col_tiles.reshape(1, SLOTS), col_tiles.reshape(SLOTS, 1)
    row_row, row_col = row_tiles.reshape(1, SLOTS), row_tiles.reshape(SLOTS, 1)

    (pay,) = call(first_sums, [sums], (col_row, right, begin), [square])
    arrived = to_all(pay)
    pos_row, pos_col, gram_r, gram_l = call(
        tables,
        [((1, SLOTS), I32), ((SLOTS, 1), I32), square, square],
        (counts, col_row, col_col, right, left),
        in_specs=[SMEM] + [VMEM] * 4,
    )
    rest, send, place_row = call(
        with_total(first_vector),
        [own, ((DEV, EXTRA, 1, TILE), F32), ((1, NAMED), I32)],
        (arrived, begin, right, gram_r, gram_l),
    )
    partial, beta_zero, grams = call(
        with_total(rows_product_first),
        [in_rows, line, ((2, TILE), F32)],
        (to_all(send), pos_col, row_row, tiles),
        work,
    )
    image, pay = call(
        image_sums_first,
        [own, ((DEV, 1, 3 * TILE), F32)],
        (in_group(partial), left, grams),
        [square],
    )
    left_one, copies, alpha_one, gram_r, gram_l = call(
        with_total(left_vector_first),
        [own, copied, line, square, square],
        (to_all(pay), image, left),
    )
    (outgoing,) = call(
        column_product, [(blocks, F32)], (in_group(copies), row_col, pos_row, tiles), work
    )
    back, pay = call(
        functools.partial(back_sums, True),
        [own, sums],
        (to_all(outgoing), right, place_row, rest, beta_zero, alpha_one),
        [square],
    )
    right_two, send, beta_one = call(
        with_total(right_vector),
        [own, (blocks, BF16), line],
        (to_all(pay), back, right, gram_r, place_row),
    )
    (partial,) = call(rows_product, [in_rows], (to_all(send), pos_col, row_row, tiles), work)
    image, pay = call(
        image_sums, [own, sums], (in_group(partial), left, left_one, beta_one), [square]
    )
    lefts, copies, alpha_two = call(
        with_total(left_vector),
        [((2, OWN * TILE), F32), copied, line],
        (to_all(pay), image, left, gram_l, left_one),
        [own],
    )
    (outgoing,) = call(
        column_product, [(blocks, F32)], (in_group(copies), row_col, pos_row, tiles), work
    )
    back, pay = call(
        functools.partial(back_sums, False),
        [own, sums],
        (to_all(outgoing), right, place_row, right_two, beta_one, alpha_two),
        [square],
    )
    rights, factors = call(
        with_total(last_vector),
        [((2, OWN * TILE), F32), ((5,), F32)],
        (to_all(pay), back, right, gram_r, right_two, beta_zero, alpha_one, beta_one, alpha_two),
        [own, line],
        out_specs=[VMEM, SMEM],
    )
    return lefts, rights, factors


def solution(mesh):
    torus = Mesh(mesh.devices.reshape(4, 4, 4, 2), ALL)
    placed = (
        P(ALL, None, None),
        P(ALL),
        P(ALL),
        P(ALL),
        P(None, ALL),
        P(None, ALL),
        P(ALL),
    )
    return jax.shard_map(
        shards,
        mesh=torus,
        in_specs=placed,
        out_specs=(P(None, ALL), P(None, ALL), P()),
        check_vma=False,
    )
```

```python
import functools

import jax
import jax.numpy as jnp
from jax import lax
from jax.experimental import pallas as pl
from jax.experimental.pallas import tpu as pltpu
from jax.sharding import Mesh
from jax.sharding import PartitionSpec as P

PEER_TILES = 8
COL = ("col_0", "col_1")
ALL = ("row_0", "row_1", "col_0", "col_1")
HIGH = lax.Precision.HIGHEST
F32, BF16, I32 = jnp.float32, jnp.bfloat16, jnp.int32

DEV = 128
OWN = 32
TILE = 128
SLOTS = 512
GROUP = 256
NAMED = DEV * PEER_TILES
PLACE = 104
PARTS = 4
CHUNK = 64
EXTRA = PEER_TILES + 3


def iota(shape, dim):
    return lax.broadcasted_iota(I32, shape, dim)


def one_hot(condition):
    return jnp.where(condition, 1.0, 0.0).astype(BF16)


def dot(a, b, ca=1, cb=0, precision=None):
    return lax.dot_general(
        a, b, (((ca,), (cb,)), ((), ())), precision=precision, preferred_element_type=F32
    )


def selected(hot, value):
    first = value.astype(BF16)
    rest = value - first.astype(F32)
    second = rest.astype(BF16)
    third = (rest - second.astype(F32)).astype(BF16)
    return dot(hot, third) + dot(hot, second) + dot(hot, first)


def products_row(basis, vector, held, copies=()):
    size = basis.shape[0]
    total = jnp.zeros((size, TILE), F32)
    for k in range(OWN):
        if copies and k % (OWN // PARTS) == 0:
            copies[k // (OWN // PARTS)].wait()
        total = total + basis[:, k * TILE : (k + 1) * TILE] * vector[k : k + 1, :]
    held[...] = jnp.zeros_like(held)
    held[0:size, :] = total
    row = dot(jnp.ones((8, TILE), F32), held[...], 1, 1, HIGH)[0:1, :]
    square = jnp.sum(vector * vector, keepdims=True)
    return jnp.where(iota((1, TILE), 1) == size, square, row)


def coefficients_of(total, size, row_total):
    lane = iota((1, TILE), 1)
    projection = jnp.where(lane < size, total, 0.0)
    square = jnp.sum(jnp.where(lane == size, total, 0.0), axis=1, keepdims=True)
    coeffs = projection / row_total
    diagonal = iota((size, TILE), 0) == iota((size, TILE), 1)
    column = jnp.sum(jnp.where(diagonal, coeffs, 0.0), axis=1, keepdims=True)
    return projection, square, coeffs, column


def subtract_basis(out, vector, basis, column):
    wide = jnp.broadcast_to(column, (column.shape[0], TILE))
    for k in range(OWN):
        part = jnp.sum(basis[:, k * TILE : (k + 1) * TILE] * wide, axis=0, keepdims=True)
        out[k : k + 1, :] = vector[k : k + 1, :] - part


def norm_of(projection, square, coeffs, column, gram, row_total):
    size = column.shape[0]
    applied = jnp.sum(gram[0:size, :] * coeffs, axis=1, keepdims=True)
    quadratic = jnp.sum(applied * column, axis=0, keepdims=True)
    linear = jnp.sum(coeffs * projection, axis=1, keepdims=True)
    left = jnp.maximum(square - 2.0 * linear + quadratic, 0.0)
    return jnp.sqrt(left / row_total + 1e-06)


def first_sums(col_hbm, basis_hbm, start_hbm, out, held, col_row, basis, start, sems):
    wide = basis.shape[1] // PARTS
    parts = [pl.ds(i * wide, wide) for i in range(PARTS)]
    copies = [pltpu.make_async_copy(col_hbm, col_row, sems.at[0])]
    copies += [pltpu.make_async_copy(start_hbm, start, sems.at[1])]
    copies += [
        pltpu.make_async_copy(basis_hbm.at[:, part], basis.at[:, part], sems.at[2 + i])
        for i, part in enumerate(parts)
    ]
    for copy in copies:
        copy.start()
    copies[0].wait()
    owner, place = col_row[...] // OWN, col_row[...] % OWN
    owners = one_hot(iota((DEV, SLOTS), 0) == owner)
    places = one_hot(iota((OWN, SLOTS), 0) == place)
    touched = dot(places, owners, 1, 1) > 0.5
    below = one_hot(iota((OWN, OWN), 1) < iota((OWN, OWN), 0))
    rank = dot(below, one_hot(touched))
    copies[1].wait()
    row = products_row(basis, start[...], held, copies[2:])
    held[...] = jnp.zeros_like(held)
    number = (iota((OWN, DEV), 0) + 1).astype(F32)
    for k in range(PEER_TILES):
        here = touched & (rank > k - 0.5) & (rank < k + 0.5)
        named = jnp.sum(jnp.where(here, number, 0.0), axis=0, keepdims=True)
        held[PLACE + k : PLACE + k + 1, :] = named - 1.0
    out[:, 0, :] = held[...].T + row


def as_column(row):
    return jnp.broadcast_to(row.astype(F32), (TILE, SLOTS)).T[:, 0:1].astype(I32)


def tables(counts, col_hbm, row_hbm, right_hbm, left_hbm, *refs):
    pos_row, pos_col, row_row, row_col, gram_r, gram_l, col_row, right, left, sems = refs
    sources = (col_hbm, row_hbm, right_hbm, left_hbm)
    targets = (col_row, row_row, right, left)
    copies = [pltpu.make_async_copy(a, b, sems.at[i]) for i, (a, b) in enumerate(zip(sources, targets))]
    for copy in copies:
        copy.start()
    count = counts[0]
    copies[0].wait()
    owner, place = col_row[...] // OWN, col_row[...] % OWN
    owners = one_hot(iota((DEV, SLOTS), 0) == owner)
    in_place = iota((OWN, SLOTS), 0) == place
    touched = one_hot(dot(one_hot(in_place), owners, 1, 1) > 0.5)
    below = one_hot(iota((OWN, OWN), 1) < iota((OWN, OWN), 0))
    rank = dot(below, touched).astype(BF16)
    mine = dot(rank, owners)
    mine = jnp.sum(jnp.where(in_place, mine, 0.0), axis=0, keepdims=True)
    position = owner * PEER_TILES + mine.astype(I32)
    position = jnp.where(iota((1, SLOTS), 1) < count, position, -1)
    pos_row[...] = position
    pos_col[...] = as_column(position)
    copies[1].wait()
    row_col[...] = as_column(row_row[...])
    for copy, basis, gram in ((copies[2], right, gram_r), (copies[3], left, gram_l)):
        copy.wait()
        size = basis.shape[0]
        gram[...] = jnp.zeros_like(gram)
        gram[0:size, 0:size] = dot(basis[...], basis[...], 1, 1, HIGH)


def place_row_of(arrived):
    lane = iota((DEV, NAMED), 0)
    spread = dot(arrived.astype(BF16), one_hot(lane - PLACE == iota((DEV, NAMED), 1) % PEER_TILES))
    own = iota((DEV, NAMED), 1) // PEER_TILES == lane
    row = jnp.sum(jnp.where(own, spread, 0.0), axis=0, keepdims=True)
    return jnp.round(row).astype(I32)


def first_vector(row_total, arrived, start_hbm, basis_hbm, gram_r, gram_l, *refs):
    rest, send, place_row, start, basis, sems = refs
    copies = [
        pltpu.make_async_copy(start_hbm, start, sems.at[0]),
        pltpu.make_async_copy(basis_hbm, basis, sems.at[1]),
    ]
    for copy in copies:
        copy.start()
    size = basis.shape[0]
    got = arrived[:, 0, :]
    total = jnp.sum(got, axis=0, keepdims=True)
    _, _, _, column = coefficients_of(total, size, row_total)
    named = place_row_of(got)
    place_row[...] = named
    for copy in copies:
        copy.wait()
    subtract_basis(rest, start, basis, column)
    vector = rest[...]
    hot = jnp.where(iota((OWN, NAMED), 0) == named, 1.0, 0.0)
    blocks = dot(hot, vector, 0, 0, HIGH).reshape(DEV, PEER_TILES, TILE)
    for k in range(PEER_TILES):
        send[:, k, 0, :] = blocks[:, k, :]
    square = jnp.sum(vector * vector, keepdims=True)
    send[:, PEER_TILES, 0, :] = jnp.broadcast_to(square, (DEV, TILE))
    send[:, PEER_TILES + 1, 0, :] = gram_r[...]
    send[:, PEER_TILES + 2, 0, :] = gram_l[...]


def tiles_times(sources, tiles, products, copies=None):
    many = 16
    row = iota((many, TILE), 0)

    def step(chunk, carry):
        if copies:
            copies(chunk).wait()
        for i in range(0, CHUNK, many):
            at = pl.multiple_of(chunk * CHUNK + i, many)
            block = tiles[pl.ds(at, many)].reshape(many * TILE, TILE)
            wide = dot(sources[pl.ds(at, many), :], block, 1, 1)
            total = wide[:, 0:TILE]
            for j in range(1, many):
                total = jnp.where(row == j, wide[:, j * TILE : (j + 1) * TILE], total)
            products[pl.ds(at, many), :] = total
        return carry

    lax.fori_loop(0, SLOTS // CHUNK, step, 0, unroll=1 if copies else 2)


def times_tiles(sources, tiles, products):
    many = 16
    row = iota((many, TILE), 0)

    def step(i, carry):
        at = pl.multiple_of(i * many, many)
        block = tiles[pl.ds(at, many)].reshape(many * TILE, TILE)
        mine = sources[pl.ds(at, many), :]
        parts = [jnp.where(row == j, mine, jnp.zeros_like(mine)) for j in range(many)]
        products[pl.ds(at, many), :] = dot(jnp.concatenate(parts, axis=1), block)
        return carry

    lax.fori_loop(0, SLOTS // many, step, 0, unroll=8)


def summed_by_row(row_row, products, out):
    rows = one_hot(iota((GROUP, SLOTS), 0) == row_row[...])
    out[...] = selected(rows, products[...]).reshape(out.shape)


def rows_product_first(
    row_total, arrived, pos_col, row_row, tiles, out, norm, grams, kept, sources, products, sems
):
    def copy(chunk):
        part = pl.ds(pl.multiple_of(chunk * CHUNK, CHUNK), CHUNK)
        return pltpu.make_async_copy(tiles.at[part], kept.at[part], sems.at[chunk])

    for chunk in range(SLOTS // CHUNK):
        copy(chunk).start()
    total = jnp.sum(arrived[:, PEER_TILES, 0, :], axis=0, keepdims=True)
    size = jnp.sqrt(total / row_total + 1e-06)
    norm[...] = size
    grams[0:1, :] = jnp.sum(arrived[:, PEER_TILES + 1, 0, :], axis=0, keepdims=True)
    grams[1:2, :] = jnp.sum(arrived[:, PEER_TILES + 2, 0, :], axis=0, keepdims=True)
    values = jnp.zeros((SLOTS, TILE), F32)
    for k in range(PEER_TILES):
        vector = (arrived[:, k, 0, :] / size).astype(BF16)
        hot = one_hot(iota((SLOTS, DEV), 1) * PEER_TILES + k == pos_col[...])
        values = values + dot(hot, vector)
    sources[...] = values.astype(BF16)
    tiles_times(sources, kept, products, copy)
    summed_by_row(row_row, products, out)


def rows_product(arrived, pos_col, row_row, tiles, out, sources, products):
    hot = one_hot(iota((SLOTS, NAMED), 1) == pos_col[...])
    vector = arrived[...].reshape(NAMED, TILE)
    sources[...] = dot(hot, vector).astype(BF16)
    tiles_times(sources, tiles, products)
    summed_by_row(row_row, products, out)


def column_product(arrived, row_col, pos_row, tiles, out, sources, products):
    hot = one_hot(iota((SLOTS, GROUP), 1) == row_col[...])
    vector = arrived[...].reshape(GROUP, TILE)
    sources[...] = dot(hot, vector).astype(BF16)
    times_tiles(sources, tiles, products)
    hot = one_hot(iota((NAMED, SLOTS), 0) == pos_row[...])
    out[...] = selected(hot, products[...]).reshape(out.shape)


def image_sums_first(arrived, basis, grams, image, out, held):
    vector = jnp.sum(arrived[...], axis=0)
    image[...] = vector
    row = products_row(basis, vector, held)
    out[:, 0, 0:TILE] = jnp.broadcast_to(row, (DEV, TILE))
    out[:, 0, TILE : 2 * TILE] = jnp.broadcast_to(grams[0:1, :], (DEV, TILE))
    out[:, 0, 2 * TILE : 3 * TILE] = jnp.broadcast_to(grams[1:2, :], (DEV, TILE))


def image_sums(arrived, basis, earlier, factor, image, out, held):
    vector = jnp.sum(arrived[...], axis=0) - factor[...] * earlier[...]
    image[...] = vector
    out[:, 0, :] = jnp.broadcast_to(products_row(basis, vector, held), (DEV, TILE))


def back_sums(divide, arrived, basis, place_row, earlier, by, factor, back, out, held):
    hot = one_hot(iota((OWN, NAMED), 0) == place_row[...])
    before = earlier[...] / by[...] if divide else earlier[...]
    vector = selected(hot, arrived[...].reshape(NAMED, TILE)) - factor[...] * before
    back[...] = vector
    out[:, 0, :] = jnp.broadcast_to(products_row(basis, vector, held), (DEV, TILE))


def left_vector_first(row_total, arrived, image, basis, new, copies, norm, gram_r, gram_l):
    got = arrived[:, 0, :]
    gram_r[...] = got[:, TILE : 2 * TILE]
    gram_l[...] = got[:, 2 * TILE : 3 * TILE]
    total = jnp.sum(got[:, 0:TILE], axis=0, keepdims=True)
    finish(row_total, total, image, basis, gram_l, new, norm)
    copies[...] = jnp.broadcast_to(new[...].astype(BF16), copies.shape)


def finish(row_total, total, vector, basis, gram, new, norm):
    size = basis.shape[0]
    projection, square, coeffs, column = coefficients_of(total, size, row_total)
    factor = norm_of(projection, square, coeffs, column, gram, row_total)
    norm[...] = jnp.broadcast_to(factor, (1, TILE))
    subtract_basis(new, vector, basis, column)
    new[...] = new[...] / factor


def lines(out, at, vector):
    for k in range(OWN):
        out[at : at + 1, k * TILE : (k + 1) * TILE] = vector[k : k + 1, :]


def left_vector(row_total, arrived, image, basis, gram, earlier, new_pair, copies, norm, new):
    total = jnp.sum(arrived[:, 0, :], axis=0, keepdims=True)
    finish(row_total, total, image, basis, gram, new, norm)
    copies[...] = jnp.broadcast_to(new[...].astype(BF16), copies.shape)
    lines(new_pair, 0, earlier)
    lines(new_pair, 1, new)


def right_vector(row_total, arrived, back, basis, gram, place_row, new, send, norm):
    total = jnp.sum(arrived[:, 0, :], axis=0, keepdims=True)
    finish(row_total, total, back, basis, gram, new, norm)
    hot = one_hot(iota((OWN, NAMED), 0) == place_row[...])
    blocks = dot(hot, new[...].astype(BF16), 0, 0)
    send[...] = blocks.astype(BF16).reshape(send.shape)


def last_vector(row_total, arrived, back, basis, gram, earlier, *rest):
    norms, (new_pair, factors, new, norm) = rest[:4], rest[4:]
    total = jnp.sum(arrived[:, 0, :], axis=0, keepdims=True)
    finish(row_total, total, back, basis, gram, new, norm)
    lines(new_pair, 0, earlier)
    lines(new_pair, 1, new)
    for i, value in enumerate((*norms, norm)):
        factors[i] = jnp.max(value[...])


VMEM = pl.BlockSpec(memory_space=pltpu.VMEM)
HBM = pl.BlockSpec(memory_space=pltpu.HBM)
SMEM = pl.BlockSpec(memory_space=pltpu.SMEM)


def in_hbm(value):
    return pltpu.with_memory_space_constraint(value, pltpu.HBM)


def call(body, outs, args, scratch=(), in_specs=None, out_specs=None, semaphores=0):
    shapes = [jax.ShapeDtypeStruct(s, d) for s, d in outs]
    return pl.pallas_call(
        body,
        out_shape=shapes,
        in_specs=in_specs or [VMEM] * len(args),
        out_specs=out_specs or [VMEM] * len(outs),
        scratch_shapes=[pltpu.VMEM(s, d) for s, d in scratch]
        + [pltpu.SemaphoreType.DMA((semaphores,))] * (semaphores > 0),
        compiler_params=pltpu.CompilerParams(vmem_limit_bytes=8 << 20),
    )(*(in_hbm(a) if spec is HBM else a for a, spec in zip(args, in_specs or args)))


def to_all(value):
    return lax.all_to_all(value, ALL, 0, 0, tiled=True)


def in_group(value):
    return lax.all_to_all(value, COL, 0, 0, tiled=True)


def shards(tiles, row_tiles, col_tiles, counts, right_basis, left_basis, start):
    row_total = float(start.shape[0] * DEV)
    with_total = lambda body: functools.partial(body, row_total)
    own = ((OWN, TILE), F32)
    line = ((1, TILE), F32)
    square = ((DEV, TILE), F32)
    sums = ((DEV, 1, TILE), F32)
    blocks = (DEV, PEER_TILES, TILE)
    in_rows = ((8, OWN, TILE), F32)
    copied = ((8, OWN, TILE), BF16)
    work = [((SLOTS, TILE), BF16), ((SLOTS, TILE), F32)]
    right, left = right_basis, left_basis
    begin = start.reshape(OWN, TILE)
    col_row, row_row = col_tiles.reshape(1, SLOTS), row_tiles.reshape(1, SLOTS)

    (pay,) = call(
        first_sums,
        [sums],
        (col_row, right, begin),
        [square, ((1, SLOTS), I32), (right.shape, F32), own],
        in_specs=[HBM] * 3,
        semaphores=2 + PARTS,
    )
    arrived = to_all(pay)
    pos_row, pos_col, row_row, row_col, gram_r, gram_l = call(
        tables,
        [((1, SLOTS), I32), ((SLOTS, 1), I32)] * 2 + [square, square],
        (counts, col_row, row_row, right, left),
        [((1, SLOTS), I32), (right.shape, F32), (left.shape, F32)],
        in_specs=[SMEM] + [HBM] * 4,
        semaphores=4,
    )
    rest, send, place_row = call(
        with_total(first_vector),
        [own, ((DEV, EXTRA, 1, TILE), F32), ((1, NAMED), I32)],
        (arrived, begin, right, gram_r, gram_l),
        [own, (right.shape, F32)],
        in_specs=[VMEM, HBM, HBM, VMEM, VMEM],
        semaphores=2,
    )
    partial, beta_zero, grams, tiles = call(
        with_total(rows_product_first),
        [in_rows, line, ((2, TILE), F32), (tiles.shape, BF16)],
        (to_all(send), pos_col, row_row, tiles),
        work,
        in_specs=[VMEM] * 3 + [HBM],
        semaphores=SLOTS // CHUNK,
    )
    image, pay = call(
        image_sums_first,
        [own, ((DEV, 1, 3 * TILE), F32)],
        (in_group(partial), left, grams),
        [square],
    )
    left_one, copies, alpha_one, gram_r, gram_l = call(
        with_total(left_vector_first),
        [own, copied, line, square, square],
        (to_all(pay), image, left),
    )
    (outgoing,) = call(
        column_product, [(blocks, F32)], (in_group(copies), row_col, pos_row, tiles), work
    )
    back, pay = call(
        functools.partial(back_sums, True),
        [own, sums],
        (to_all(outgoing), right, place_row, rest, beta_zero, alpha_one),
        [square],
    )
    right_two, send, beta_one = call(
        with_total(right_vector),
        [own, (blocks, BF16), line],
        (to_all(pay), back, right, gram_r, place_row),
    )
    (partial,) = call(rows_product, [in_rows], (to_all(send), pos_col, row_row, tiles), work)
    image, pay = call(
        image_sums, [own, sums], (in_group(partial), left, left_one, beta_one), [square]
    )
    lefts, copies, alpha_two = call(
        with_total(left_vector),
        [((2, OWN * TILE), F32), copied, line],
        (to_all(pay), image, left, gram_l, left_one),
        [own],
    )
    (outgoing,) = call(
        column_product, [(blocks, F32)], (in_group(copies), row_col, pos_row, tiles), work
    )
    back, pay = call(
        functools.partial(back_sums, False),
        [own, sums],
        (to_all(outgoing), right, place_row, right_two, beta_one, alpha_two),
        [square],
    )
    rights, factors = call(
        with_total(last_vector),
        [((2, OWN * TILE), F32), ((5,), F32)],
        (to_all(pay), back, right, gram_r, right_two, beta_zero, alpha_one, beta_one, alpha_two),
        [own, line],
        out_specs=[VMEM, SMEM],
    )
    return lefts, rights, factors


def solution(mesh):
    torus = Mesh(mesh.devices.reshape(4, 4, 4, 2), ALL)
    placed = (
        P(ALL, None, None),
        P(ALL),
        P(ALL),
        P(ALL),
        P(None, ALL),
        P(None, ALL),
        P(ALL),
    )
    return jax.shard_map(
        shards,
        mesh=torus,
        in_specs=placed,
        out_specs=(P(None, ALL), P(None, ALL), P()),
        check_vma=False,
    )
```

```python
import functools

import jax
import jax.numpy as jnp
from jax import lax
from jax.experimental import pallas as pl
from jax.experimental.pallas import tpu as pltpu
from jax.sharding import Mesh
from jax.sharding import PartitionSpec as P

PEER_TILES = 8
COL = ("col_0", "col_1")
ALL = ("row_0", "row_1", "col_0", "col_1")
HIGH = lax.Precision.HIGHEST
F32, BF16, I32 = jnp.float32, jnp.bfloat16, jnp.int32

DEV = 128
OWN = 32
TILE = 128
SLOTS = 512
GROUP = 256
NAMED = DEV * PEER_TILES
PLACE = 104
PARTS = 4
CHUNK = 64
EXTRA = PEER_TILES + 3


def iota(shape, dim):
    return lax.broadcasted_iota(I32, shape, dim)


def one_hot(condition):
    return jnp.where(condition, 1.0, 0.0).astype(BF16)


def dot(a, b, ca=1, cb=0, precision=None):
    return lax.dot_general(
        a, b, (((ca,), (cb,)), ((), ())), precision=precision, preferred_element_type=F32
    )


def selected(hot, value):
    first = value.astype(BF16)
    rest = value - first.astype(F32)
    second = rest.astype(BF16)
    third = (rest - second.astype(F32)).astype(BF16)
    return dot(hot, third) + dot(hot, second) + dot(hot, first)


def products_row(basis, vector, held, copies=()):
    size = basis.shape[0]
    total = jnp.zeros((size, TILE), F32)
    for k in range(OWN):
        if copies and k % (OWN // PARTS) == 0:
            copies[k // (OWN // PARTS)].wait()
        total = total + basis[:, k * TILE : (k + 1) * TILE] * vector[k : k + 1, :]
    held[...] = jnp.zeros_like(held)
    held[0:size, :] = total
    row = dot(jnp.ones((8, TILE), F32), held[...], 1, 1, HIGH)[0:1, :]
    square = jnp.sum(vector * vector, keepdims=True)
    return jnp.where(iota((1, TILE), 1) == size, square, row)


def coefficients_of(total, size, row_total):
    lane = iota((1, TILE), 1)
    projection = jnp.where(lane < size, total, 0.0)
    square = jnp.sum(jnp.where(lane == size, total, 0.0), axis=1, keepdims=True)
    coeffs = projection / row_total
    diagonal = iota((size, TILE), 0) == iota((size, TILE), 1)
    column = jnp.sum(jnp.where(diagonal, coeffs, 0.0), axis=1, keepdims=True)
    return projection, square, coeffs, column


def subtract_basis(out, vector, basis, column):
    wide = jnp.broadcast_to(column, (column.shape[0], TILE))
    for k in range(OWN):
        part = jnp.sum(basis[:, k * TILE : (k + 1) * TILE] * wide, axis=0, keepdims=True)
        out[k : k + 1, :] = vector[k : k + 1, :] - part


def norm_of(projection, square, coeffs, column, gram, row_total):
    size = column.shape[0]
    applied = jnp.sum(gram[0:size, :] * coeffs, axis=1, keepdims=True)
    quadratic = jnp.sum(applied * column, axis=0, keepdims=True)
    linear = jnp.sum(coeffs * projection, axis=1, keepdims=True)
    left = jnp.maximum(square - 2.0 * linear + quadratic, 0.0)
    return jnp.sqrt(left / row_total + 1e-06)


def first_sums(col_hbm, basis_hbm, start_hbm, out, rank, col_row, start, basis, held, sems):
    wide = basis.shape[1] // PARTS
    parts = [pl.ds(i * wide, wide) for i in range(PARTS)]
    copies = [pltpu.make_async_copy(col_hbm, col_row, sems.at[0])]
    copies += [pltpu.make_async_copy(start_hbm, start, sems.at[1])]
    copies += [
        pltpu.make_async_copy(basis_hbm.at[:, part], basis.at[:, part], sems.at[2 + i])
        for i, part in enumerate(parts)
    ]
    for copy in copies:
        copy.start()
    copies[0].wait()
    owner, place = col_row[...] // OWN, col_row[...] % OWN
    owners = one_hot(iota((DEV, SLOTS), 0) == owner)
    places = one_hot(iota((OWN, SLOTS), 0) == place)
    touched = dot(places, owners, 1, 1) > 0.5
    below = one_hot(iota((OWN, OWN), 1) < iota((OWN, OWN), 0))
    places = dot(below, one_hot(touched))
    rank[...] = places.astype(BF16)
    copies[1].wait()
    row = products_row(basis, start[...], held, copies[2:])
    held[...] = jnp.zeros_like(held)
    number = (iota((OWN, DEV), 0) + 1).astype(F32)
    for k in range(PEER_TILES):
        here = touched & (places > k - 0.5) & (places < k + 0.5)
        named = jnp.sum(jnp.where(here, number, 0.0), axis=0, keepdims=True)
        held[PLACE + k : PLACE + k + 1, :] = named - 1.0
    out[:, 0, :] = held[...].T + row


def gram_of(basis):
    value = basis[...]
    first = value.astype(BF16)
    rest = value - first.astype(F32)
    second = rest.astype(BF16)
    third = (rest - second.astype(F32)).astype(BF16)
    low = dot(third, first, 1, 1)
    middle = dot(second, first, 1, 1)
    both = low + middle
    return dot(second, second, 1, 1) + (both + both.T) + dot(first, first, 1, 1)


def tables(counts, rank, col_row, right, row_hbm, left_hbm, *refs):
    pos_row, pos_col, row_row, row_col, gram_r, gram_l, left, sems = refs
    copies = [
        pltpu.make_async_copy(left_hbm, left, sems.at[0]),
        pltpu.make_async_copy(row_hbm, row_row, sems.at[1]),
    ]
    for copy in copies:
        copy.start()
    for basis, gram in ((right, gram_r), (left, gram_l)):
        if basis is left:
            copies[0].wait()
        size = basis.shape[0]
        gram[...] = jnp.zeros_like(gram)
        gram[0:size, 0:size] = gram_of(basis)
    copies[1].wait()
    count = counts[0]
    owner, place = col_row[...] // OWN, col_row[...] % OWN
    owners = one_hot(iota((DEV, SLOTS), 0) == owner)
    mine = dot(rank[...], owners)
    mine = jnp.where(iota((OWN, SLOTS), 0) == place, mine, 0.0)
    position = owner * PEER_TILES + jnp.sum(mine, axis=0, keepdims=True).astype(I32)
    position = jnp.where(iota((1, SLOTS), 1) < count, position, -1)
    pos_row[...] = position
    both = jnp.where(iota((8, SLOTS), 0) == 0, position, row_row[...])
    columns = both.astype(F32).T.astype(I32)
    pos_col[...] = columns[:, 0:1]
    row_col[...] = columns[:, 1:2]


def place_row_of(arrived):
    lane = iota((DEV, NAMED), 0)
    spread = dot(arrived.astype(BF16), one_hot(lane - PLACE == iota((DEV, NAMED), 1) % PEER_TILES))
    own = iota((DEV, NAMED), 1) // PEER_TILES == lane
    row = jnp.sum(jnp.where(own, spread, 0.0), axis=0, keepdims=True)
    return jnp.round(row).astype(I32)


def first_vector(row_total, arrived, start, basis, gram_r, gram_l, rest, send, place_row):
    size = basis.shape[0]
    got = arrived[:, 0, :]
    total = jnp.sum(got, axis=0, keepdims=True)
    _, _, _, column = coefficients_of(total, size, row_total)
    named = place_row_of(got)
    place_row[...] = named
    subtract_basis(rest, start, basis, column)
    vector = rest[...]
    hot = jnp.where(iota((OWN, NAMED), 0) == named, 1.0, 0.0)
    blocks = dot(hot, vector, 0, 0, HIGH).reshape(DEV, PEER_TILES, TILE)
    for k in range(PEER_TILES):
        send[:, k, 0, :] = blocks[:, k, :]
    square = jnp.sum(vector * vector, keepdims=True)
    send[:, PEER_TILES, 0, :] = jnp.broadcast_to(square, (DEV, TILE))
    send[:, PEER_TILES + 1, 0, :] = gram_r[...]
    send[:, PEER_TILES + 2, 0, :] = gram_l[...]


def tiles_times(sources, tiles, products, copies=None):
    many = 16
    row = iota((many, TILE), 0)

    def step(chunk, carry):
        if copies:
            copies(chunk).wait()
        for i in range(0, CHUNK, many):
            at = pl.multiple_of(chunk * CHUNK + i, many)
            block = tiles[pl.ds(at, many)].reshape(many * TILE, TILE)
            wide = dot(sources[pl.ds(at, many), :], block, 1, 1)
            total = wide[:, 0:TILE]
            for j in range(1, many):
                total = jnp.where(row == j, wide[:, j * TILE : (j + 1) * TILE], total)
            products[pl.ds(at, many), :] = total
        return carry

    lax.fori_loop(0, SLOTS // CHUNK, step, 0, unroll=1 if copies else 2)


def times_tiles(sources, tiles, products):
    many = 16
    row = iota((many, TILE), 0)

    def step(i, carry):
        at = pl.multiple_of(i * many, many)
        block = tiles[pl.ds(at, many)].reshape(many * TILE, TILE)
        mine = sources[pl.ds(at, many), :]
        parts = [jnp.where(row == j, mine, jnp.zeros_like(mine)) for j in range(many)]
        products[pl.ds(at, many), :] = dot(jnp.concatenate(parts, axis=1), block)
        return carry

    lax.fori_loop(0, SLOTS // many, step, 0, unroll=8)


def summed_by_row(row_row, products, out):
    rows = one_hot(iota((GROUP, SLOTS), 0) == row_row[...])
    out[...] = selected(rows, products[...]).reshape(out.shape)


def rows_product_first(
    row_total, arrived, pos_col, row_row, tiles, out, norm, grams, kept, sources, products, sems
):
    def copy(chunk):
        part = pl.ds(pl.multiple_of(chunk * CHUNK, CHUNK), CHUNK)
        return pltpu.make_async_copy(tiles.at[part], kept.at[part], sems.at[chunk])

    for chunk in range(SLOTS // CHUNK):
        copy(chunk).start()
    total = jnp.sum(arrived[:, PEER_TILES, 0, :], axis=0, keepdims=True)
    size = jnp.sqrt(total / row_total + 1e-06)
    norm[...] = size
    grams[0:1, :] = jnp.sum(arrived[:, PEER_TILES + 1, 0, :], axis=0, keepdims=True)
    grams[1:2, :] = jnp.sum(arrived[:, PEER_TILES + 2, 0, :], axis=0, keepdims=True)
    values = jnp.zeros((SLOTS, TILE), F32)
    for k in range(PEER_TILES):
        vector = (arrived[:, k, 0, :] / size).astype(BF16)
        hot = one_hot(iota((SLOTS, DEV), 1) * PEER_TILES + k == pos_col[...])
        values = values + dot(hot, vector)
    sources[...] = values.astype(BF16)
    tiles_times(sources, kept, products, copy)
    summed_by_row(row_row, products, out)


def rows_product(arrived, pos_col, row_row, tiles, out, sources, products):
    hot = one_hot(iota((SLOTS, NAMED), 1) == pos_col[...])
    vector = arrived[...].reshape(NAMED, TILE)
    sources[...] = dot(hot, vector).astype(BF16)
    tiles_times(sources, tiles, products)
    summed_by_row(row_row, products, out)


def column_product(arrived, row_col, pos_row, tiles, out, sources, products):
    hot = one_hot(iota((SLOTS, GROUP), 1) == row_col[...])
    vector = arrived[...].reshape(GROUP, TILE)
    sources[...] = dot(hot, vector).astype(BF16)
    times_tiles(sources, tiles, products)
    hot = one_hot(iota((NAMED, SLOTS), 0) == pos_row[...])
    out[...] = selected(hot, products[...]).reshape(out.shape)


def image_sums_first(arrived, basis, grams, image, out, held):
    vector = jnp.sum(arrived[...], axis=0)
    image[...] = vector
    row = products_row(basis, vector, held)
    out[:, 0, 0:TILE] = jnp.broadcast_to(row, (DEV, TILE))
    out[:, 0, TILE : 2 * TILE] = jnp.broadcast_to(grams[0:1, :], (DEV, TILE))
    out[:, 0, 2 * TILE : 3 * TILE] = jnp.broadcast_to(grams[1:2, :], (DEV, TILE))


def image_sums(arrived, basis, earlier, factor, image, out, held):
    vector = jnp.sum(arrived[...], axis=0) - factor[...] * earlier[...]
    image[...] = vector
    out[:, 0, :] = jnp.broadcast_to(products_row(basis, vector, held), (DEV, TILE))


def back_sums(divide, arrived, basis, place_row, earlier, by, factor, back, out, held):
    hot = one_hot(iota((OWN, NAMED), 0) == place_row[...])
    before = earlier[...] / by[...] if divide else earlier[...]
    vector = selected(hot, arrived[...].reshape(NAMED, TILE)) - factor[...] * before
    back[...] = vector
    out[:, 0, :] = jnp.broadcast_to(products_row(basis, vector, held), (DEV, TILE))


def left_vector_first(row_total, arrived, image, basis, new, copies, norm, gram_r, gram_l):
    got = arrived[:, 0, :]
    gram_r[...] = got[:, TILE : 2 * TILE]
    gram_l[...] = got[:, 2 * TILE : 3 * TILE]
    total = jnp.sum(got[:, 0:TILE], axis=0, keepdims=True)
    finish(row_total, total, image, basis, gram_l, new, norm)
    copies[...] = jnp.broadcast_to(new[...].astype(BF16), copies.shape)


def finish(row_total, total, vector, basis, gram, new, norm):
    size = basis.shape[0]
    projection, square, coeffs, column = coefficients_of(total, size, row_total)
    factor = norm_of(projection, square, coeffs, column, gram, row_total)
    norm[...] = jnp.broadcast_to(factor, (1, TILE))
    subtract_basis(new, vector, basis, column)
    new[...] = new[...] / factor


def lines(out, at, vector):
    for k in range(OWN):
        out[at : at + 1, k * TILE : (k + 1) * TILE] = vector[k : k + 1, :]


def left_vector(row_total, arrived, image, basis, gram, earlier, new_pair, copies, norm, new):
    total = jnp.sum(arrived[:, 0, :], axis=0, keepdims=True)
    finish(row_total, total, image, basis, gram, new, norm)
    copies[...] = jnp.broadcast_to(new[...].astype(BF16), copies.shape)
    lines(new_pair, 0, earlier)
    lines(new_pair, 1, new)


def right_vector(row_total, arrived, back, basis, gram, place_row, new, send, norm):
    total = jnp.sum(arrived[:, 0, :], axis=0, keepdims=True)
    finish(row_total, total, back, basis, gram, new, norm)
    hot = one_hot(iota((OWN, NAMED), 0) == place_row[...])
    blocks = dot(hot, new[...].astype(BF16), 0, 0)
    send[...] = blocks.astype(BF16).reshape(send.shape)


def last_vector(row_total, arrived, back, basis, gram, earlier, *rest):
    norms, (new_pair, factors, new, norm) = rest[:4], rest[4:]
    total = jnp.sum(arrived[:, 0, :], axis=0, keepdims=True)
    finish(row_total, total, back, basis, gram, new, norm)
    lines(new_pair, 0, earlier)
    lines(new_pair, 1, new)
    for i, value in enumerate((*norms, norm)):
        factors[i] = jnp.max(value[...])


VMEM = pl.BlockSpec(memory_space=pltpu.VMEM)
HBM = pl.BlockSpec(memory_space=pltpu.HBM)
SMEM = pl.BlockSpec(memory_space=pltpu.SMEM)


def in_hbm(value):
    return pltpu.with_memory_space_constraint(value, pltpu.HBM)


def call(body, outs, args, scratch=(), in_specs=None, out_specs=None, semaphores=0):
    shapes = [jax.ShapeDtypeStruct(s, d) for s, d in outs]
    return pl.pallas_call(
        body,
        out_shape=shapes,
        in_specs=in_specs or [VMEM] * len(args),
        out_specs=out_specs or [VMEM] * len(outs),
        scratch_shapes=[pltpu.VMEM(s, d) for s, d in scratch]
        + [pltpu.SemaphoreType.DMA((semaphores,))] * (semaphores > 0),
        compiler_params=pltpu.CompilerParams(vmem_limit_bytes=8 << 20),
    )(*(in_hbm(a) if spec is HBM else a for a, spec in zip(args, in_specs or args)))


def to_all(value):
    return lax.all_to_all(value, ALL, 0, 0, tiled=True)


def in_group(value):
    return lax.all_to_all(value, COL, 0, 0, tiled=True)


def shards(tiles, row_tiles, col_tiles, counts, right_basis, left_basis, start):
    row_total = float(start.shape[0] * DEV)
    with_total = lambda body: functools.partial(body, row_total)
    own = ((OWN, TILE), F32)
    line = ((1, TILE), F32)
    square = ((DEV, TILE), F32)
    sums = ((DEV, 1, TILE), F32)
    blocks = (DEV, PEER_TILES, TILE)
    in_rows = ((8, OWN, TILE), F32)
    copied = ((8, OWN, TILE), BF16)
    work = [((SLOTS, TILE), BF16), ((SLOTS, TILE), F32)]
    right, left = right_basis, left_basis
    begin = start.reshape(OWN, TILE)
    col_row, row_row = col_tiles.reshape(1, SLOTS), row_tiles.reshape(1, SLOTS)

    pay, rank, col_row, begin, right = call(
        first_sums,
        [sums, ((OWN, DEV), BF16), ((1, SLOTS), I32), own, (right.shape, F32)],
        (col_row, right, begin),
        [square],
        in_specs=[HBM] * 3,
        semaphores=2 + PARTS,
    )
    arrived = to_all(pay)
    pos_row, pos_col, row_row, row_col, gram_r, gram_l = call(
        tables,
        [((1, SLOTS), I32), ((SLOTS, 1), I32)] * 2 + [square, square],
        (counts, rank, col_row, right, row_row, left),
        [(left.shape, F32)],
        in_specs=[SMEM] + [VMEM] * 3 + [HBM] * 2,
        semaphores=2,
    )
    rest, send, place_row = call(
        with_total(first_vector),
        [own, ((DEV, EXTRA, 1, TILE), F32), ((1, NAMED), I32)],
        (arrived, begin, right, gram_r, gram_l),
    )
    partial, beta_zero, grams, tiles = call(
        with_total(rows_product_first),
        [in_rows, line, ((2, TILE), F32), (tiles.shape, BF16)],
        (to_all(send), pos_col, row_row, tiles),
        work,
        in_specs=[VMEM] * 3 + [HBM],
        semaphores=SLOTS // CHUNK,
    )
    image, pay = call(
        image_sums_first,
        [own, ((DEV, 1, 3 * TILE), F32)],
        (in_group(partial), left, grams),
        [square],
    )
    left_one, copies, alpha_one, gram_r, gram_l = call(
        with_total(left_vector_first),
        [own, copied, line, square, square],
        (to_all(pay), image, left),
    )
    (outgoing,) = call(
        column_product, [(blocks, F32)], (in_group(copies), row_col, pos_row, tiles), work
    )
    back, pay = call(
        functools.partial(back_sums, True),
        [own, sums],
        (to_all(outgoing), right, place_row, rest, beta_zero, alpha_one),
        [square],
    )
    right_two, send, beta_one = call(
        with_total(right_vector),
        [own, (blocks, BF16), line],
        (to_all(pay), back, right, gram_r, place_row),
    )
    (partial,) = call(rows_product, [in_rows], (to_all(send), pos_col, row_row, tiles), work)
    image, pay = call(
        image_sums, [own, sums], (in_group(partial), left, left_one, beta_one), [square]
    )
    lefts, copies, alpha_two = call(
        with_total(left_vector),
        [((2, OWN * TILE), F32), copied, line],
        (to_all(pay), image, left, gram_l, left_one),
        [own],
    )
    (outgoing,) = call(
        column_product, [(blocks, F32)], (in_group(copies), row_col, pos_row, tiles), work
    )
    back, pay = call(
        functools.partial(back_sums, False),
        [own, sums],
        (to_all(outgoing), right, place_row, right_two, beta_one, alpha_two),
        [square],
    )
    rights, factors = call(
        with_total(last_vector),
        [((2, OWN * TILE), F32), ((5,), F32)],
        (to_all(pay), back, right, gram_r, right_two, beta_zero, alpha_one, beta_one, alpha_two),
        [own, line],
        out_specs=[VMEM, SMEM],
    )
    return lefts, rights, factors


def solution(mesh):
    torus = Mesh(mesh.devices.reshape(4, 4, 4, 2), ALL)
    placed = (
        P(ALL, None, None),
        P(ALL),
        P(ALL),
        P(ALL),
        P(None, ALL),
        P(None, ALL),
        P(ALL),
    )
    return jax.shard_map(
        shards,
        mesh=torus,
        in_specs=placed,
        out_specs=(P(None, ALL), P(None, ALL), P()),
        check_vma=False,
    )
```

```python
import functools

import jax
import jax.numpy as jnp
from jax import lax
from jax.experimental import pallas as pl
from jax.experimental.pallas import tpu as pltpu
from jax.sharding import Mesh
from jax.sharding import PartitionSpec as P

PEER_TILES = 8
ALL = ("row_0", "row_1", "col_0", "col_1")
SEND_ALL = ("col_1", "col_0", "row_1", "row_0")
SEND_COL = ("col_1", "col_0")
HIGH = lax.Precision.HIGHEST
F32, BF16, I32 = jnp.float32, jnp.bfloat16, jnp.int32

DEV = 128
OWN = 32
TILE = 128
SLOTS = 512
GROUP = 256
NAMED = DEV * PEER_TILES
PLACE = 104
PARTS = 4
CHUNK = 64
AHEAD = 4
EXTRA = PEER_TILES + 3


def iota(shape, dim):
    return lax.broadcasted_iota(I32, shape, dim)


def block_of(device):
    near = (device % 2) * 64 + (device // 2 % 4) * 16
    return near + (device // 8 % 4) * 4 + device // 32


def group_row_of(row):
    owner = row // OWN
    return ((owner % 2) * 4 + owner // 2) * OWN + row % OWN


def one_hot(condition):
    return jnp.where(condition, 1.0, 0.0).astype(BF16)


def dot(a, b, ca=1, cb=0, precision=None):
    return lax.dot_general(
        a, b, (((ca,), (cb,)), ((), ())), precision=precision, preferred_element_type=F32
    )


def selected(hot, value):
    first = value.astype(BF16)
    rest = value - first.astype(F32)
    second = rest.astype(BF16)
    third = (rest - second.astype(F32)).astype(BF16)
    return dot(hot, third) + dot(hot, second) + dot(hot, first)


def products_row(basis, vector, held, copies=()):
    size = basis.shape[0]
    total = jnp.zeros((size, TILE), F32)
    for k in range(OWN):
        if copies and k % (OWN // PARTS) == 0:
            copies[k // (OWN // PARTS)].wait()
        total = total + basis[:, k * TILE : (k + 1) * TILE] * vector[k : k + 1, :]
    held[...] = jnp.zeros_like(held)
    held[0:size, :] = total
    row = dot(jnp.ones((8, TILE), F32), held[...], 1, 1, HIGH)[0:1, :]
    square = jnp.sum(vector * vector, keepdims=True)
    return jnp.where(iota((1, TILE), 1) == size, square, row)


def coefficients_of(total, size, row_total):
    lane = iota((1, TILE), 1)
    projection = jnp.where(lane < size, total, 0.0)
    square = jnp.sum(jnp.where(lane == size, total, 0.0), axis=1, keepdims=True)
    coeffs = projection / row_total
    diagonal = iota((size, TILE), 0) == iota((size, TILE), 1)
    column = jnp.sum(jnp.where(diagonal, coeffs, 0.0), axis=1, keepdims=True)
    return projection, square, coeffs, column


def subtract_basis(out, vector, basis, column):
    wide = jnp.broadcast_to(column, (column.shape[0], TILE))
    for k in range(OWN):
        part = jnp.sum(basis[:, k * TILE : (k + 1) * TILE] * wide, axis=0, keepdims=True)
        out[k : k + 1, :] = vector[k : k + 1, :] - part


def norm_of(projection, square, coeffs, column, gram, row_total):
    size = column.shape[0]
    applied = jnp.sum(gram[0:size, :] * coeffs, axis=1, keepdims=True)
    quadratic = jnp.sum(applied * column, axis=0, keepdims=True)
    linear = jnp.sum(coeffs * projection, axis=1, keepdims=True)
    left = jnp.maximum(square - 2.0 * linear + quadratic, 0.0)
    return jnp.sqrt(left / row_total + 1e-06)


def first_sums(col_hbm, basis_hbm, start_hbm, out, rank, col_row, start, basis, held, sems):
    wide = basis.shape[1] // PARTS
    parts = [pl.ds(i * wide, wide) for i in range(PARTS)]
    copies = [pltpu.make_async_copy(col_hbm, col_row, sems.at[0])]
    copies += [pltpu.make_async_copy(start_hbm, start, sems.at[1])]
    copies += [
        pltpu.make_async_copy(basis_hbm.at[:, part], basis.at[:, part], sems.at[2 + i])
        for i, part in enumerate(parts)
    ]
    for copy in copies:
        copy.start()
    copies[0].wait()
    owner, place = block_of(col_row[...] // OWN), col_row[...] % OWN
    owners = one_hot(iota((DEV, SLOTS), 0) == owner)
    places = one_hot(iota((OWN, SLOTS), 0) == place)
    touched = dot(places, owners, 1, 1) > 0.5
    below = one_hot(iota((OWN, OWN), 1) < iota((OWN, OWN), 0))
    places = dot(below, one_hot(touched))
    rank[...] = places.astype(BF16)
    copies[1].wait()
    row = products_row(basis, start[...], held, copies[2:])
    held[...] = jnp.zeros_like(held)
    number = (iota((OWN, DEV), 0) + 1).astype(F32)
    for k in range(PEER_TILES):
        here = touched & (places > k - 0.5) & (places < k + 0.5)
        named = jnp.sum(jnp.where(here, number, 0.0), axis=0, keepdims=True)
        held[PLACE + k : PLACE + k + 1, :] = named - 1.0
    out[:, 0, :] = held[...].T + row


def gram_of(basis):
    value = basis[...]
    first = value.astype(BF16)
    rest = value - first.astype(F32)
    second = rest.astype(BF16)
    third = (rest - second.astype(F32)).astype(BF16)
    low = dot(third, first, 1, 1)
    middle = dot(second, first, 1, 1)
    both = low + middle
    return dot(second, second, 1, 1) + (both + both.T) + dot(first, first, 1, 1)


def tables(counts, rank, col_row, right, row_hbm, left_hbm, *refs):
    pos_row, pos_col, row_row, row_col, gram_r, gram_l, left, given_row, sems = refs
    copies = [
        pltpu.make_async_copy(left_hbm, left, sems.at[0]),
        pltpu.make_async_copy(row_hbm, given_row, sems.at[1]),
    ]
    for copy in copies:
        copy.start()
    for basis, gram in ((right, gram_r), (left, gram_l)):
        if basis is left:
            copies[0].wait()
        size = basis.shape[0]
        gram[...] = jnp.zeros_like(gram)
        gram[0:size, 0:size] = gram_of(basis)
    copies[1].wait()
    row = group_row_of(given_row[...])
    row_row[...] = row
    count = counts[0]
    owner, place = block_of(col_row[...] // OWN), col_row[...] % OWN
    owners = one_hot(iota((DEV, SLOTS), 0) == owner)
    mine = dot(rank[...], owners)
    mine = jnp.where(iota((OWN, SLOTS), 0) == place, mine, 0.0)
    position = owner * PEER_TILES + jnp.sum(mine, axis=0, keepdims=True).astype(I32)
    position = jnp.where(iota((1, SLOTS), 1) < count, position, -1)
    pos_row[...] = position
    both = jnp.where(iota((8, SLOTS), 0) == 0, position, row)
    columns = both.astype(F32).T.astype(I32)
    pos_col[...] = columns[:, 0:1]
    row_col[...] = columns[:, 1:2]


def place_row_of(arrived):
    lane = iota((DEV, NAMED), 0)
    spread = dot(arrived.astype(BF16), one_hot(lane - PLACE == iota((DEV, NAMED), 1) % PEER_TILES))
    own = iota((DEV, NAMED), 1) // PEER_TILES == lane
    row = jnp.sum(jnp.where(own, spread, 0.0), axis=0, keepdims=True)
    return jnp.round(row).astype(I32)


def first_vector(row_total, arrived, start, basis, gram_r, gram_l, rest, send, place_row):
    size = basis.shape[0]
    got = arrived[:, 0, :]
    total = jnp.sum(got, axis=0, keepdims=True)
    _, _, _, column = coefficients_of(total, size, row_total)
    named = place_row_of(got)
    place_row[...] = named
    subtract_basis(rest, start, basis, column)
    vector = rest[...]
    hot = jnp.where(iota((OWN, NAMED), 0) == named, 1.0, 0.0)
    blocks = dot(hot, vector, 0, 0, HIGH).reshape(DEV, PEER_TILES, TILE)
    for k in range(PEER_TILES):
        send[:, k, 0, :] = blocks[:, k, :]
    square = jnp.sum(vector * vector, keepdims=True)
    send[:, PEER_TILES, 0, :] = jnp.broadcast_to(square, (DEV, TILE))
    send[:, PEER_TILES + 1, 0, :] = gram_r[...]
    send[:, PEER_TILES + 2, 0, :] = gram_l[...]


def tiles_times(sources, tiles, products, copies=None):
    many = 16
    row = iota((many, TILE), 0)

    for at in range(0, SLOTS, many):
        if copies and at % CHUNK == 0:
            copies[at // CHUNK].wait()
            for copy in copies[at // CHUNK + AHEAD : at // CHUNK + AHEAD + 1]:
                copy.start()
        block = tiles[pl.ds(at, many)].reshape(many * TILE, TILE)
        wide = dot(sources[pl.ds(at, many), :], block, 1, 1)
        total = wide[:, 0:TILE]
        for j in range(1, many):
            total = jnp.where(row == j, wide[:, j * TILE : (j + 1) * TILE], total)
        products[pl.ds(at, many), :] = total


def times_tiles(sources, tiles, products):
    many = 16
    row = iota((many, TILE), 0)

    def step(i, carry):
        at = pl.multiple_of(i * many, many)
        block = tiles[pl.ds(at, many)].reshape(many * TILE, TILE)
        mine = sources[pl.ds(at, many), :]
        parts = [jnp.where(row == j, mine, jnp.zeros_like(mine)) for j in range(many)]
        products[pl.ds(at, many), :] = dot(jnp.concatenate(parts, axis=1), block)
        return carry

    lax.fori_loop(0, SLOTS // many, step, 0, unroll=True)


def summed_by_row(row_row, products, out):
    rows = one_hot(iota((GROUP, SLOTS), 0) == row_row[...])
    out[...] = selected(rows, products[...]).reshape(out.shape)


def rows_product_first(
    row_total, arrived, pos_col, row_row, tiles, out, norm, grams, kept, sources, products, sems
):
    parts = [pl.ds(at, CHUNK) for at in range(0, SLOTS, CHUNK)]
    copies = [
        pltpu.make_async_copy(tiles.at[part], kept.at[part], sems.at[i])
        for i, part in enumerate(parts)
    ]
    for copy in copies[:AHEAD]:
        copy.start()
    part = lambda k: arrived[pl.ds(k, DEV, stride=EXTRA), :]
    add = lambda k: jnp.sum(part(PEER_TILES + k), axis=0, keepdims=True)
    size = jnp.sqrt(add(0) / row_total + 1e-06)
    norm[...] = size
    grams[0:1, :] = add(1)
    grams[1:2, :] = add(2)
    values = jnp.zeros((SLOTS, TILE), F32)
    position = pos_col[...]
    for k in range(PEER_TILES):
        vector = (part(k) / size).astype(BF16)
        hot = one_hot(iota((SLOTS, DEV), 1) * PEER_TILES + k == position)
        values = values + dot(hot, vector)
    sources[...] = values.astype(BF16)
    tiles_times(sources, kept, products, copies)
    summed_by_row(row_row, products, out)


def rows_product(arrived, pos_col, row_row, tiles, out, sources, products):
    hot = one_hot(iota((SLOTS, NAMED), 1) == pos_col[...])
    vector = arrived[...].reshape(NAMED, TILE)
    sources[...] = dot(hot, vector).astype(BF16)
    tiles_times(sources, tiles, products)
    summed_by_row(row_row, products, out)


def column_product(arrived, row_col, pos_row, tiles, out, sources, products):
    hot = one_hot(iota((SLOTS, GROUP), 1) == row_col[...])
    vector = arrived[...].reshape(GROUP, TILE)
    sources[...] = dot(hot, vector).astype(BF16)
    times_tiles(sources, tiles, products)
    hot = one_hot(iota((NAMED, SLOTS), 0) == pos_row[...])
    out[...] = selected(hot, products[...]).reshape(out.shape)


def image_sums_first(arrived, basis, grams, image, out, held):
    vector = jnp.sum(arrived[...], axis=0)
    image[...] = vector
    row = products_row(basis, vector, held)
    out[:, 0, 0:TILE] = jnp.broadcast_to(row, (DEV, TILE))
    out[:, 0, TILE : 2 * TILE] = jnp.broadcast_to(grams[0:1, :], (DEV, TILE))
    out[:, 0, 2 * TILE : 3 * TILE] = jnp.broadcast_to(grams[1:2, :], (DEV, TILE))


def image_sums(arrived, basis, earlier, factor, image, out, held):
    vector = jnp.sum(arrived[...], axis=0) - factor[...] * earlier[...]
    image[...] = vector
    out[:, 0, :] = jnp.broadcast_to(products_row(basis, vector, held), (DEV, TILE))


def back_sums(divide, arrived, basis, place_row, earlier, by, factor, back, out, held):
    hot = one_hot(iota((OWN, NAMED), 0) == place_row[...])
    before = earlier[...] / by[...] if divide else earlier[...]
    vector = selected(hot, arrived[...].reshape(NAMED, TILE)) - factor[...] * before
    back[...] = vector
    out[:, 0, :] = jnp.broadcast_to(products_row(basis, vector, held), (DEV, TILE))


def left_vector_first(row_total, arrived, image, basis, new, copies, norm, gram_r, gram_l):
    got = arrived[:, 0, :]
    gram_r[...] = got[:, TILE : 2 * TILE]
    gram_l[...] = got[:, 2 * TILE : 3 * TILE]
    total = jnp.sum(got[:, 0:TILE], axis=0, keepdims=True)
    finish(row_total, total, image, basis, gram_l, new, norm)
    copies[...] = jnp.broadcast_to(new[...].astype(BF16), copies.shape)


def finish(row_total, total, vector, basis, gram, new, norm):
    size = basis.shape[0]
    projection, square, coeffs, column = coefficients_of(total, size, row_total)
    factor = norm_of(projection, square, coeffs, column, gram, row_total)
    norm[...] = jnp.broadcast_to(factor, (1, TILE))
    subtract_basis(new, vector, basis, column)
    new[...] = new[...] / factor


def lines(out, at, vector):
    for k in range(OWN):
        out[at : at + 1, k * TILE : (k + 1) * TILE] = vector[k : k + 1, :]


def left_vector(row_total, arrived, image, basis, gram, earlier, new_pair, copies, norm, new):
    total = jnp.sum(arrived[:, 0, :], axis=0, keepdims=True)
    finish(row_total, total, image, basis, gram, new, norm)
    copies[...] = jnp.broadcast_to(new[...].astype(BF16), copies.shape)
    lines(new_pair, 0, earlier)
    lines(new_pair, 1, new)


def right_vector(row_total, arrived, back, basis, gram, place_row, new, send, norm):
    total = jnp.sum(arrived[:, 0, :], axis=0, keepdims=True)
    finish(row_total, total, back, basis, gram, new, norm)
    hot = one_hot(iota((OWN, NAMED), 0) == place_row[...])
    blocks = dot(hot, new[...].astype(BF16), 0, 0)
    send[...] = blocks.astype(BF16).reshape(send.shape)


def last_vector(row_total, arrived, back, basis, gram, earlier, *rest):
    norms, (new_pair, factors, new, norm) = rest[:4], rest[4:]
    total = jnp.sum(arrived[:, 0, :], axis=0, keepdims=True)
    finish(row_total, total, back, basis, gram, new, norm)
    lines(new_pair, 0, earlier)
    lines(new_pair, 1, new)
    for i, value in enumerate((*norms, norm)):
        factors[i] = jnp.max(value[...])


VMEM = pl.BlockSpec(memory_space=pltpu.VMEM)
HBM = pl.BlockSpec(memory_space=pltpu.HBM)
SMEM = pl.BlockSpec(memory_space=pltpu.SMEM)


def in_hbm(value):
    return pltpu.with_memory_space_constraint(value, pltpu.HBM)


def call(body, outs, args, scratch=(), in_specs=None, out_specs=None, semaphores=0):
    shapes = [jax.ShapeDtypeStruct(s, d) for s, d in outs]
    return pl.pallas_call(
        body,
        out_shape=shapes,
        in_specs=in_specs or [VMEM] * len(args),
        out_specs=out_specs or [VMEM] * len(outs),
        scratch_shapes=[pltpu.VMEM(s, d) for s, d in scratch]
        + [pltpu.SemaphoreType.DMA((semaphores,))] * (semaphores > 0),
        compiler_params=pltpu.CompilerParams(vmem_limit_bytes=8 << 20),
    )(*(in_hbm(a) if spec is HBM else a for a, spec in zip(args, in_specs or args)))


def to_all(value):
    return lax.all_to_all(value, SEND_ALL, 0, 0, tiled=True)


def in_group(value):
    return lax.all_to_all(value, SEND_COL, 0, 0, tiled=True)


def shards(tiles, row_tiles, col_tiles, counts, right_basis, left_basis, start):
    row_total = float(start.shape[0] * DEV)
    with_total = lambda body: functools.partial(body, row_total)
    own = ((OWN, TILE), F32)
    line = ((1, TILE), F32)
    square = ((DEV, TILE), F32)
    sums = ((DEV, 1, TILE), F32)
    blocks = (DEV, PEER_TILES, TILE)
    in_rows = ((8, OWN, TILE), F32)
    copied = ((8, OWN, TILE), BF16)
    work = [((SLOTS, TILE), BF16), ((SLOTS, TILE), F32)]
    right, left = right_basis, left_basis
    begin = start.reshape(OWN, TILE)
    col_row, row_row = col_tiles.reshape(1, SLOTS), row_tiles.reshape(1, SLOTS)

    pay, rank, col_row, begin, right = call(
        first_sums,
        [sums, ((OWN, DEV), BF16), ((1, SLOTS), I32), own, (right.shape, F32)],
        (col_row, right, begin),
        [square],
        in_specs=[HBM] * 3,
        semaphores=2 + PARTS,
    )
    arrived = to_all(pay)
    pos_row, pos_col, row_row, row_col, gram_r, gram_l = call(
        tables,
        [((1, SLOTS), I32), ((SLOTS, 1), I32)] * 2 + [square, square],
        (counts, rank, col_row, right, row_row, left),
        [(left.shape, F32), ((1, SLOTS), I32)],
        in_specs=[SMEM] + [VMEM] * 3 + [HBM] * 2,
        semaphores=2,
    )
    rest, send, place_row = call(
        with_total(first_vector),
        [own, ((DEV, EXTRA, 1, TILE), F32), ((1, NAMED), I32)],
        (arrived, begin, right, gram_r, gram_l),
    )
    partial, beta_zero, grams, tiles = call(
        with_total(rows_product_first),
        [in_rows, line, ((2, TILE), F32), (tiles.shape, BF16)],
        (to_all(send).reshape(DEV * EXTRA, TILE), pos_col, row_row, tiles),
        work,
        in_specs=[VMEM] * 3 + [HBM],
        semaphores=SLOTS // CHUNK,
    )
    image, pay = call(
        image_sums_first,
        [own, ((DEV, 1, 3 * TILE), F32)],
        (in_group(partial), left, grams),
        [square],
    )
    left_one, copies, alpha_one, gram_r, gram_l = call(
        with_total(left_vector_first),
        [own, copied, line, square, square],
        (to_all(pay), image, left),
    )
    (outgoing,) = call(
        column_product, [(blocks, F32)], (in_group(copies), row_col, pos_row, tiles), work
    )
    back, pay = call(
        functools.partial(back_sums, True),
        [own, sums],
        (to_all(outgoing), right, place_row, rest, beta_zero, alpha_one),
        [square],
    )
    right_two, send, beta_one = call(
        with_total(right_vector),
        [own, (blocks, BF16), line],
        (to_all(pay), back, right, gram_r, place_row),
    )
    (partial,) = call(rows_product, [in_rows], (to_all(send), pos_col, row_row, tiles), work)
    image, pay = call(
        image_sums, [own, sums], (in_group(partial), left, left_one, beta_one), [square]
    )
    lefts, copies, alpha_two = call(
        with_total(left_vector),
        [((2, OWN * TILE), F32), copied, line],
        (to_all(pay), image, left, gram_l, left_one),
        [own],
    )
    (outgoing,) = call(
        column_product, [(blocks, F32)], (in_group(copies), row_col, pos_row, tiles), work
    )
    back, pay = call(
        functools.partial(back_sums, False),
        [own, sums],
        (to_all(outgoing), right, place_row, right_two, beta_one, alpha_two),
        [square],
    )
    rights, factors = call(
        with_total(last_vector),
        [((2, OWN * TILE), F32), ((5,), F32)],
        (to_all(pay), back, right, gram_r, right_two, beta_zero, alpha_one, beta_one, alpha_two),
        [own, line],
        out_specs=[VMEM, SMEM],
    )
    return lefts, rights, factors


def solution(mesh):
    torus = Mesh(mesh.devices.reshape(4, 4, 4, 2), ALL)
    placed = (
        P(ALL, None, None),
        P(ALL),
        P(ALL),
        P(ALL),
        P(None, ALL),
        P(None, ALL),
        P(ALL),
    )
    return jax.shard_map(
        shards,
        mesh=torus,
        in_specs=placed,
        out_specs=(P(None, ALL), P(None, ALL), P()),
        check_vma=False,
    )
```

```python
import functools

import jax
import jax.numpy as jnp
from jax import lax
from jax.experimental import pallas as pl
from jax.experimental.pallas import tpu as pltpu
from jax.sharding import Mesh
from jax.sharding import PartitionSpec as P

PEER_TILES = 8
ALL = ("row_0", "row_1", "col_0", "col_1")
SEND_ALL = ("col_1", "col_0", "row_1", "row_0")
SEND_COL = ("col_1", "col_0")
HIGH = lax.Precision.HIGHEST
F32, BF16, I32 = jnp.float32, jnp.bfloat16, jnp.int32

DEV = 128
OWN = 32
TILE = 128
SLOTS = 512
GROUP = 256
NAMED = DEV * PEER_TILES
PLACE = 104
PARTS = 4
SQUARE, DIAGONAL = 126, 127
EXTRA = PEER_TILES + 1


def iota(shape, dim):
    return lax.broadcasted_iota(I32, shape, dim)


def block_of(device):
    near = (device % 2) * 64 + (device // 2 % 4) * 16
    return near + (device // 8 % 4) * 4 + device // 32


def group_row_of(row):
    owner = row // OWN
    return ((owner % 2) * 4 + owner // 2) * OWN + row % OWN


def one_hot(condition):
    return jnp.where(condition, 1.0, 0.0).astype(BF16)


def dot(a, b, ca=1, cb=0, precision=None):
    return lax.dot_general(
        a, b, (((ca,), (cb,)), ((), ())), precision=precision, preferred_element_type=F32
    )


def selected(hot, value):
    first = value.astype(BF16)
    rest = value - first.astype(F32)
    second = rest.astype(BF16)
    third = (rest - second.astype(F32)).astype(BF16)
    return dot(hot, third) + dot(hot, second) + dot(hot, first)


def products_row(basis, vector, held, copies=()):
    size = basis.shape[0]
    total = jnp.zeros((size, TILE), F32)
    for k in range(OWN):
        if copies and k % (OWN // PARTS) == 0:
            copies[k // (OWN // PARTS)].wait()
        total = total + basis[:, k * TILE : (k + 1) * TILE] * vector[k : k + 1, :]
    held[...] = jnp.zeros_like(held)
    held[0:size, :] = total
    row = dot(jnp.ones((8, TILE), F32), held[...], 1, 1, HIGH)[0:1, :]
    square = jnp.sum(vector * vector, keepdims=True)
    return jnp.where(iota((1, TILE), 1) == size, square, row)


def coefficients_of(total, size, row_total):
    lane = iota((1, TILE), 1)
    projection = jnp.where(lane < size, total, 0.0)
    square = jnp.sum(jnp.where(lane == size, total, 0.0), axis=1, keepdims=True)
    coeffs = projection / row_total
    diagonal = iota((size, TILE), 0) == iota((size, TILE), 1)
    column = jnp.sum(jnp.where(diagonal, coeffs, 0.0), axis=1, keepdims=True)
    return projection, square, coeffs, column


def subtract_basis(out, vector, basis, column):
    wide = jnp.broadcast_to(column, (column.shape[0], TILE))
    for k in range(OWN):
        part = jnp.sum(basis[:, k * TILE : (k + 1) * TILE] * wide, axis=0, keepdims=True)
        out[k : k + 1, :] = vector[k : k + 1, :] - part


def norm_of(projection, square, coeffs, column, gram, row_total):
    size = column.shape[0]
    applied = jnp.sum(gram[0:size, :] * coeffs, axis=1, keepdims=True)
    quadratic = jnp.sum(applied * column, axis=0, keepdims=True)
    linear = jnp.sum(coeffs * projection, axis=1, keepdims=True)
    left = jnp.maximum(square - 2.0 * linear + quadratic, 0.0)
    return jnp.sqrt(left / row_total + 1e-06)


def first_sums(col_hbm, basis_hbm, start_hbm, out, rank, col_row, start, basis, held, sems):
    wide = basis.shape[1] // PARTS
    parts = [pl.ds(i * wide, wide) for i in range(PARTS)]
    copies = [pltpu.make_async_copy(col_hbm, col_row, sems.at[0])]
    copies += [pltpu.make_async_copy(start_hbm, start, sems.at[1])]
    copies += [
        pltpu.make_async_copy(basis_hbm.at[:, part], basis.at[:, part], sems.at[2 + i])
        for i, part in enumerate(parts)
    ]
    for copy in copies:
        copy.start()
    copies[0].wait()
    owner, place = block_of(col_row[...] // OWN), col_row[...] % OWN
    owners = one_hot(iota((DEV, SLOTS), 0) == owner)
    places = one_hot(iota((OWN, SLOTS), 0) == place)
    touched = dot(places, owners, 1, 1) > 0.5
    below = one_hot(iota((OWN, OWN), 1) < iota((OWN, OWN), 0))
    places = dot(below, one_hot(touched))
    rank[...] = places.astype(BF16)
    copies[1].wait()
    row = products_row(basis, start[...], held, copies[2:])
    held[...] = jnp.zeros_like(held)
    number = (iota((OWN, DEV), 0) + 1).astype(F32)
    for k in range(PEER_TILES):
        here = touched & (places > k - 0.5) & (places < k + 0.5)
        named = jnp.sum(jnp.where(here, number, 0.0), axis=0, keepdims=True)
        held[PLACE + k : PLACE + k + 1, :] = named - 1.0
    out[:, 0, :] = held[...].T + row


def gram_of(basis):
    value = basis[...]
    first = value.astype(BF16)
    rest = value - first.astype(F32)
    second = rest.astype(BF16)
    third = (rest - second.astype(F32)).astype(BF16)
    low = dot(third, first, 1, 1)
    middle = dot(second, first, 1, 1)
    both = low + middle
    return dot(second, second, 1, 1) + (both + both.T) + dot(first, first, 1, 1)


def tables(counts, rank, col_row, right, row_hbm, left_hbm, *refs):
    pos_row, pos_col, row_row, row_col, gram_r, gram_l, left, given_row, sems = refs
    copies = [
        pltpu.make_async_copy(left_hbm, left, sems.at[0]),
        pltpu.make_async_copy(row_hbm, given_row, sems.at[1]),
    ]
    for copy in copies:
        copy.start()
    for basis, gram in ((right, gram_r), (left, gram_l)):
        if basis is left:
            copies[0].wait()
        size = basis.shape[0]
        gram[...] = jnp.zeros_like(gram)
        gram[0:size, 0:size] = gram_of(basis)
    copies[1].wait()
    row = group_row_of(given_row[...])
    row_row[...] = row
    count = counts[0]
    owner, place = block_of(col_row[...] // OWN), col_row[...] % OWN
    owners = one_hot(iota((DEV, SLOTS), 0) == owner)
    mine = dot(rank[...], owners)
    mine = jnp.where(iota((OWN, SLOTS), 0) == place, mine, 0.0)
    position = owner * PEER_TILES + jnp.sum(mine, axis=0, keepdims=True).astype(I32)
    position = jnp.where(iota((1, SLOTS), 1) < count, position, -1)
    pos_row[...] = position
    both = jnp.where(iota((8, SLOTS), 0) == 0, position, row)
    columns = both.astype(F32).T.astype(I32)
    pos_col[...] = columns[:, 0:1]
    row_col[...] = columns[:, 1:2]


def place_row_of(arrived):
    lane = iota((DEV, NAMED), 0)
    spread = dot(arrived.astype(BF16), one_hot(lane - PLACE == iota((DEV, NAMED), 1) % PEER_TILES))
    own = iota((DEV, NAMED), 1) // PEER_TILES == lane
    row = jnp.sum(jnp.where(own, spread, 0.0), axis=0, keepdims=True)
    return jnp.round(row).astype(I32)


def first_vector(row_total, arrived, start, basis, gram_r, gram_l, _, rest, send, place_row):
    size = basis.shape[0]
    got = arrived[:, 0, :]
    total = jnp.sum(got, axis=0, keepdims=True)
    _, _, _, column = coefficients_of(total, size, row_total)
    named = place_row_of(got)
    place_row[...] = named
    subtract_basis(rest, start, basis, column)
    vector = rest[...]
    hot = jnp.where(iota((OWN, NAMED), 0) == named, 1.0, 0.0)
    blocks = dot(hot, vector, 0, 0, HIGH).reshape(DEV, PEER_TILES, TILE)
    for k in range(PEER_TILES):
        send[:, k, 0, :] = blocks[:, k, :]
    square = jnp.sum(vector * vector, keepdims=True)
    row, lane = iota((DEV, TILE), 0), iota((DEV, TILE), 1)
    diagonal = jnp.sum(jnp.where(row == lane, gram_r[...], 0.0), axis=1, keepdims=True)
    packed = jnp.where(row > lane, gram_r[...], gram_l[...])
    packed = jnp.where(lane == DIAGONAL, diagonal, packed)
    send[:, PEER_TILES, 0, :] = jnp.where(lane == SQUARE, square, packed)


def tiles_times(sources, tiles, products):
    many = 16
    row = iota((many, TILE), 0)

    for at in range(0, SLOTS, many):
        block = tiles[pl.ds(at, many)].reshape(many * TILE, TILE)
        wide = dot(sources[pl.ds(at, many), :], block, 1, 1)
        total = wide[:, 0:TILE]
        for j in range(1, many):
            total = jnp.where(row == j, wide[:, j * TILE : (j + 1) * TILE], total)
        products[pl.ds(at, many), :] = total


def times_tiles(sources, tiles, products):
    many = 16
    row = iota((many, TILE), 0)

    def step(i, carry):
        at = pl.multiple_of(i * many, many)
        block = tiles[pl.ds(at, many)].reshape(many * TILE, TILE)
        mine = sources[pl.ds(at, many), :]
        parts = [jnp.where(row == j, mine, jnp.zeros_like(mine)) for j in range(many)]
        products[pl.ds(at, many), :] = dot(jnp.concatenate(parts, axis=1), block)
        return carry

    lax.fori_loop(0, SLOTS // many, step, 0, unroll=True)


def summed_by_row(row_row, products, out):
    rows = one_hot(iota((GROUP, SLOTS), 0) == row_row[...])
    out[...] = selected(rows, products[...]).reshape(out.shape)


def rows_product_first(
    row_total, arrived, pos_col, row_row, tiles, out, norm, gram_row, sources, products
):
    part = lambda k: arrived[pl.ds(k, DEV, stride=EXTRA), :]
    total = jnp.sum(part(PEER_TILES), axis=0, keepdims=True)
    gram_row[...] = total
    total = jnp.sum(jnp.where(iota((1, TILE), 1) == SQUARE, total, 0.0), axis=1, keepdims=True)
    size = jnp.sqrt(total / row_total + 1e-06)
    norm[...] = jnp.broadcast_to(size, (1, TILE))
    values = jnp.zeros((SLOTS, TILE), F32)
    position = pos_col[...]
    for k in range(PEER_TILES):
        vector = (part(k) / size).astype(BF16)
        hot = one_hot(iota((SLOTS, DEV), 1) * PEER_TILES + k == position)
        values = values + dot(hot, vector)
    sources[...] = values.astype(BF16)
    tiles_times(sources, tiles, products)
    summed_by_row(row_row, products, out)


def rows_product(arrived, pos_col, row_row, tiles, out, sources, products):
    hot = one_hot(iota((SLOTS, NAMED), 1) == pos_col[...])
    vector = arrived[...].reshape(NAMED, TILE)
    sources[...] = dot(hot, vector).astype(BF16)
    tiles_times(sources, tiles, products)
    summed_by_row(row_row, products, out)


def column_product(arrived, row_col, pos_row, tiles, out, sources, products):
    hot = one_hot(iota((SLOTS, GROUP), 1) == row_col[...])
    vector = arrived[...].reshape(GROUP, TILE)
    sources[...] = dot(hot, vector).astype(BF16)
    times_tiles(sources, tiles, products)
    hot = one_hot(iota((NAMED, SLOTS), 0) == pos_row[...])
    out[...] = selected(hot, products[...]).reshape(out.shape)


def image_sums_first(arrived, basis, gram_row, image, out, held):
    vector = jnp.sum(arrived[...], axis=0)
    image[...] = vector
    row = products_row(basis, vector, held)
    out[:, 0, 0:TILE] = jnp.broadcast_to(row, (DEV, TILE))
    out[:, 0, TILE : 2 * TILE] = jnp.broadcast_to(gram_row[...], (DEV, TILE))


def image_sums(arrived, basis, earlier, factor, image, out, held):
    vector = jnp.sum(arrived[...], axis=0) - factor[...] * earlier[...]
    image[...] = vector
    out[:, 0, :] = jnp.broadcast_to(products_row(basis, vector, held), (DEV, TILE))


def back_sums(divide, arrived, basis, place_row, earlier, by, factor, back, out, held):
    hot = one_hot(iota((OWN, NAMED), 0) == place_row[...])
    before = earlier[...] / by[...] if divide else earlier[...]
    vector = selected(hot, arrived[...].reshape(NAMED, TILE)) - factor[...] * before
    back[...] = vector
    out[:, 0, :] = jnp.broadcast_to(products_row(basis, vector, held), (DEV, TILE))


def left_vector_first(row_total, arrived, image, basis, new, copies, norm, gram_r, gram_l):
    got = arrived[:, 0, :]
    both = got[:, TILE : 2 * TILE]
    row, lane = iota((DEV, TILE), 0), iota((DEV, TILE), 1)
    diagonal = jnp.sum(jnp.where(lane == DIAGONAL, both, 0.0), axis=1, keepdims=True)
    gram_r[...] = jnp.where(row > lane, both + both, jnp.where(row == lane, diagonal, 0.0))
    upper = jnp.where(row < lane, both + both, jnp.where(row == lane, both, 0.0))
    gram_l[...] = jnp.where(lane < basis.shape[0], upper, 0.0)
    total = jnp.sum(got[:, 0:TILE], axis=0, keepdims=True)
    finish(row_total, total, image, basis, gram_l, new, norm)
    copies[...] = jnp.broadcast_to(new[...].astype(BF16), copies.shape)


def finish(row_total, total, vector, basis, gram, new, norm):
    size = basis.shape[0]
    projection, square, coeffs, column = coefficients_of(total, size, row_total)
    factor = norm_of(projection, square, coeffs, column, gram, row_total)
    norm[...] = jnp.broadcast_to(factor, (1, TILE))
    subtract_basis(new, vector, basis, column)
    new[...] = new[...] / factor


def left_vector(row_total, arrived, image, basis, gram, new, copies, norm):
    total = jnp.sum(arrived[:, 0, :], axis=0, keepdims=True)
    finish(row_total, total, image, basis, gram, new, norm)
    copies[...] = jnp.broadcast_to(new[...].astype(BF16), copies.shape)


def right_vector(row_total, arrived, back, basis, gram, place_row, new, send, norm):
    total = jnp.sum(arrived[:, 0, :], axis=0, keepdims=True)
    finish(row_total, total, back, basis, gram, new, norm)
    hot = one_hot(iota((OWN, NAMED), 0) == place_row[...])
    blocks = dot(hot, new[...].astype(BF16), 0, 0)
    send[...] = blocks.astype(BF16).reshape(send.shape)


def last_vector(row_total, arrived, back, basis, gram, earlier, left_one, left_two, *rest):
    norms, (left_pair, new_pair, factors, new, norm) = rest[:4], rest[4:]
    left_pair[:, 0, :] = left_one[...]
    left_pair[:, 1, :] = left_two[...]
    total = jnp.sum(arrived[:, 0, :], axis=0, keepdims=True)
    finish(row_total, total, back, basis, gram, new, norm)
    new_pair[:, 0, :] = earlier[...]
    new_pair[:, 1, :] = new[...]
    for i, value in enumerate((*norms, norm)):
        factors[i] = jnp.max(value[...])


VMEM = pl.BlockSpec(memory_space=pltpu.VMEM)
HBM = pl.BlockSpec(memory_space=pltpu.HBM)
SMEM = pl.BlockSpec(memory_space=pltpu.SMEM)


def in_hbm(value):
    return pltpu.with_memory_space_constraint(value, pltpu.HBM)


def call(body, outs, args, scratch=(), in_specs=None, out_specs=None, semaphores=0):
    shapes = [jax.ShapeDtypeStruct(s, d) for s, d in outs]
    return pl.pallas_call(
        body,
        out_shape=shapes,
        in_specs=in_specs or [VMEM] * len(args),
        out_specs=out_specs or [VMEM] * len(outs),
        scratch_shapes=[pltpu.VMEM(s, d) for s, d in scratch]
        + [pltpu.SemaphoreType.DMA((semaphores,))] * (semaphores > 0),
        compiler_params=pltpu.CompilerParams(vmem_limit_bytes=8 << 20),
    )(*(in_hbm(a) if spec is HBM else a for a, spec in zip(args, in_specs or args)))


def to_all(value):
    return lax.all_to_all(value, SEND_ALL, 0, 0, tiled=True)


def in_group(value):
    return lax.all_to_all(value, SEND_COL, 0, 0, tiled=True)


def shards(tiles, row_tiles, col_tiles, counts, right_basis, left_basis, start):
    row_total = float(start.shape[0] * DEV)
    with_total = lambda body: functools.partial(body, row_total)
    own = ((OWN, TILE), F32)
    line = ((1, TILE), F32)
    square = ((DEV, TILE), F32)
    sums = ((DEV, 1, TILE), F32)
    blocks = (DEV, PEER_TILES, TILE)
    in_rows = ((8, OWN, TILE), F32)
    copied = ((8, OWN, TILE), BF16)
    work = [((SLOTS, TILE), BF16), ((SLOTS, TILE), F32)]
    right, left = right_basis, left_basis
    begin = start.reshape(OWN, TILE)
    col_row, row_row = col_tiles.reshape(1, SLOTS), row_tiles.reshape(1, SLOTS)

    pay, rank, col_row, begin, right = call(
        first_sums,
        [sums, ((OWN, DEV), BF16), ((1, SLOTS), I32), own, (right.shape, F32)],
        (col_row, right, begin),
        [square],
        in_specs=[HBM] * 3,
        semaphores=2 + PARTS,
    )
    arrived = to_all(pay)
    pos_row, pos_col, row_row, row_col, gram_r, gram_l = call(
        tables,
        [((1, SLOTS), I32), ((SLOTS, 1), I32)] * 2 + [square, square],
        (counts, rank, col_row, right, row_row, left),
        [(left.shape, F32), ((1, SLOTS), I32)],
        in_specs=[SMEM] + [VMEM] * 3 + [HBM] * 2,
        semaphores=2,
    )
    rest, send, place_row = call(
        with_total(first_vector),
        [own, ((DEV, EXTRA, 1, TILE), F32), ((1, NAMED), I32)],
        (arrived, begin, right, gram_r, gram_l, tiles),
        in_specs=[VMEM] * 5 + [HBM],
    )
    partial, beta_zero, gram_row = call(
        with_total(rows_product_first),
        [in_rows, line, line],
        (to_all(send).reshape(DEV * EXTRA, TILE), pos_col, row_row, tiles),
        work,
    )
    image, pay = call(
        image_sums_first,
        [own, ((DEV, 1, 2 * TILE), F32)],
        (in_group(partial), left, gram_row),
        [square],
    )
    left_one, copies, alpha_one, gram_r, gram_l = call(
        with_total(left_vector_first),
        [own, copied, line, square, square],
        (to_all(pay), image, left),
    )
    (outgoing,) = call(
        column_product, [(blocks, F32)], (in_group(copies), row_col, pos_row, tiles), work
    )
    back, pay = call(
        functools.partial(back_sums, True),
        [own, sums],
        (to_all(outgoing), right, place_row, rest, beta_zero, alpha_one),
        [square],
    )
    right_two, send, beta_one = call(
        with_total(right_vector),
        [own, (blocks, BF16), line],
        (to_all(pay), back, right, gram_r, place_row),
    )
    (partial,) = call(rows_product, [in_rows], (to_all(send), pos_col, row_row, tiles), work)
    image, pay = call(
        image_sums, [own, sums], (in_group(partial), left, left_one, beta_one), [square]
    )
    left_two, copies, alpha_two = call(
        with_total(left_vector), [own, copied, line], (to_all(pay), image, left, gram_l)
    )
    (outgoing,) = call(
        column_product, [(blocks, F32)], (in_group(copies), row_col, pos_row, tiles), work
    )
    back, pay = call(
        functools.partial(back_sums, False),
        [own, sums],
        (to_all(outgoing), right, place_row, right_two, beta_one, alpha_two),
        [square],
    )
    norms = (beta_zero, alpha_one, beta_one, alpha_two)
    lefts, rights, factors = call(
        with_total(last_vector),
        [((OWN, 2, TILE), F32)] * 2 + [((5,), F32)],
        (to_all(pay), back, right, gram_r, right_two, left_one, left_two, *norms),
        [own, line],
        out_specs=[VMEM, VMEM, SMEM],
    )
    as_rows = lambda pair: pair.transpose(1, 0, 2).reshape(2, OWN * TILE)
    return as_rows(lefts), as_rows(rights), factors


def solution(mesh):
    torus = Mesh(mesh.devices.reshape(4, 4, 4, 2), ALL)
    placed = (
        P(ALL, None, None),
        P(ALL),
        P(ALL),
        P(ALL),
        P(None, ALL),
        P(None, ALL),
        P(ALL),
    )
    return jax.shard_map(
        shards,
        mesh=torus,
        in_specs=placed,
        out_specs=(P(None, ALL), P(None, ALL), P()),
        check_vma=False,
    )
```

```python
import functools

import jax
import jax.numpy as jnp
from jax import lax
from jax.experimental import pallas as pl
from jax.experimental.pallas import tpu as pltpu
from jax.sharding import Mesh
from jax.sharding import PartitionSpec as P

PEER_TILES = 8
ALL = ("row_0", "row_1", "col_0", "col_1")
SEND_ALL = ("col_1", "col_0", "row_1", "row_0")
SEND_COL = ("col_1", "col_0")
HIGH = lax.Precision.HIGHEST
F32, BF16, I32 = jnp.float32, jnp.bfloat16, jnp.int32

DEV = 128
OWN = 32
TILE = 128
SLOTS = 512
GROUP = 256
NAMED = DEV * PEER_TILES
PLACE = 104
PARTS = 4
SQUARE, DIAGONAL = 126, 127
EXTRA = PEER_TILES + 1


def iota(shape, dim):
    return lax.broadcasted_iota(I32, shape, dim)


def block_of(device):
    near = (device % 2) * 64 + (device // 2 % 4) * 16
    return near + (device // 8 % 4) * 4 + device // 32


def group_row_of(row):
    owner = row // OWN
    return ((owner % 2) * 4 + owner // 2) * OWN + row % OWN


def one_hot(condition):
    return jnp.where(condition, 1.0, 0.0).astype(BF16)


def dot(a, b, ca=1, cb=0, precision=None):
    return lax.dot_general(
        a, b, (((ca,), (cb,)), ((), ())), precision=precision, preferred_element_type=F32
    )


def selected(hot, value):
    first = value.astype(BF16)
    rest = value - first.astype(F32)
    second = rest.astype(BF16)
    third = (rest - second.astype(F32)).astype(BF16)
    return dot(hot, third) + dot(hot, second) + dot(hot, first)


def products_row(basis, vector, held, copies=()):
    size = basis.shape[0]
    total = jnp.zeros((size, TILE), F32)
    for k in range(OWN):
        if copies and k % (OWN // PARTS) == 0:
            copies[k // (OWN // PARTS)].wait()
        total = total + basis[:, k * TILE : (k + 1) * TILE] * vector[k : k + 1, :]
    held[...] = jnp.zeros_like(held)
    held[0:size, :] = total
    row = dot(jnp.ones((8, TILE), F32), held[...], 1, 1, HIGH)[0:1, :]
    square = jnp.sum(vector * vector, keepdims=True)
    return jnp.where(iota((1, TILE), 1) == size, square, row)


def coefficients_of(total, size, row_total):
    lane = iota((1, TILE), 1)
    projection = jnp.where(lane < size, total, 0.0)
    square = jnp.sum(jnp.where(lane == size, total, 0.0), axis=1, keepdims=True)
    coeffs = projection / row_total
    diagonal = iota((size, TILE), 0) == iota((size, TILE), 1)
    column = jnp.sum(jnp.where(diagonal, coeffs, 0.0), axis=1, keepdims=True)
    return projection, square, coeffs, column


def subtract_basis(out, vector, basis, column):
    wide = jnp.broadcast_to(column, (column.shape[0], TILE))
    for k in range(OWN):
        part = jnp.sum(basis[:, k * TILE : (k + 1) * TILE] * wide, axis=0, keepdims=True)
        out[k : k + 1, :] = vector[k : k + 1, :] - part


def norm_of(projection, square, coeffs, column, gram, row_total):
    size = column.shape[0]
    applied = jnp.sum(gram[0:size, :] * coeffs, axis=1, keepdims=True)
    quadratic = jnp.sum(applied * column, axis=0, keepdims=True)
    linear = jnp.sum(coeffs * projection, axis=1, keepdims=True)
    left = jnp.maximum(square - 2.0 * linear + quadratic, 0.0)
    return jnp.sqrt(left / row_total + 1e-06)


def first_sums(col_hbm, basis_hbm, start_hbm, out, rank, col_row, start, basis, held, sems):
    wide = basis.shape[1] // PARTS
    parts = [pl.ds(i * wide, wide) for i in range(PARTS)]
    copies = [pltpu.make_async_copy(col_hbm, col_row, sems.at[0])]
    copies += [pltpu.make_async_copy(start_hbm, start, sems.at[1])]
    copies += [
        pltpu.make_async_copy(basis_hbm.at[:, part], basis.at[:, part], sems.at[2 + i])
        for i, part in enumerate(parts)
    ]
    for copy in copies:
        copy.start()
    copies[0].wait()
    owner, place = block_of(col_row[...] // OWN), col_row[...] % OWN
    owners = one_hot(iota((DEV, SLOTS), 0) == owner)
    places = one_hot(iota((OWN, SLOTS), 0) == place)
    touched = dot(places, owners, 1, 1) > 0.5
    below = one_hot(iota((OWN, OWN), 1) < iota((OWN, OWN), 0))
    places = dot(below, one_hot(touched))
    rank[...] = places.astype(BF16)
    copies[1].wait()
    row = products_row(basis, start[...], held, copies[2:])
    held[...] = jnp.zeros_like(held)
    number = (iota((OWN, DEV), 0) + 1).astype(F32)
    for k in range(PEER_TILES):
        here = touched & (places > k - 0.5) & (places < k + 0.5)
        named = jnp.sum(jnp.where(here, number, 0.0), axis=0, keepdims=True)
        held[PLACE + k : PLACE + k + 1, :] = named - 1.0
    out[:, 0, :] = held[...].T + row


def gram_of(basis):
    value = basis[...]
    first = value.astype(BF16)
    rest = value - first.astype(F32)
    second = rest.astype(BF16)
    third = (rest - second.astype(F32)).astype(BF16)
    low = dot(third, first, 1, 1)
    middle = dot(second, first, 1, 1)
    both = low + middle
    return dot(second, second, 1, 1) + (both + both.T) + dot(first, first, 1, 1)


def tables(counts, rank, col_row, right, row_hbm, left_hbm, *refs):
    pos_row, pos_col, row_row, row_col, gram_r, gram_l, left, given_row, sems = refs
    copies = [
        pltpu.make_async_copy(left_hbm, left, sems.at[0]),
        pltpu.make_async_copy(row_hbm, given_row, sems.at[1]),
    ]
    for copy in copies:
        copy.start()
    for basis, gram in ((right, gram_r), (left, gram_l)):
        if basis is left:
            copies[0].wait()
        size = basis.shape[0]
        gram[...] = jnp.zeros_like(gram)
        gram[0:size, 0:size] = gram_of(basis)
    copies[1].wait()
    row = group_row_of(given_row[...])
    row_row[...] = row
    count = counts[0]
    owner, place = block_of(col_row[...] // OWN), col_row[...] % OWN
    owners = one_hot(iota((DEV, SLOTS), 0) == owner)
    mine = dot(rank[...], owners)
    mine = jnp.where(iota((OWN, SLOTS), 0) == place, mine, 0.0)
    position = owner * PEER_TILES + jnp.sum(mine, axis=0, keepdims=True).astype(I32)
    position = jnp.where(iota((1, SLOTS), 1) < count, position, -1)
    pos_row[...] = position
    both = jnp.where(iota((8, SLOTS), 0) == 0, position, row)
    columns = both.astype(F32).T.astype(I32)
    pos_col[...] = columns[:, 0:1]
    row_col[...] = columns[:, 1:2]


def place_row_of(arrived):
    lane = iota((DEV, NAMED), 0)
    spread = dot(arrived.astype(BF16), one_hot(lane - PLACE == iota((DEV, NAMED), 1) % PEER_TILES))
    own = iota((DEV, NAMED), 1) // PEER_TILES == lane
    row = jnp.sum(jnp.where(own, spread, 0.0), axis=0, keepdims=True)
    return jnp.round(row).astype(I32)


def first_vector(row_total, arrived, start, basis, gram_r, gram_l, _, rest, send, place_row):
    size = basis.shape[0]
    got = arrived[:, 0, :]
    total = jnp.sum(got, axis=0, keepdims=True)
    _, _, _, column = coefficients_of(total, size, row_total)
    named = place_row_of(got)
    place_row[...] = named
    subtract_basis(rest, start, basis, column)
    vector = rest[...]
    hot = jnp.where(iota((OWN, NAMED), 0) == named, 1.0, 0.0)
    blocks = dot(hot, vector, 0, 0, HIGH).reshape(DEV, PEER_TILES, TILE)
    for k in range(PEER_TILES):
        send[:, k, 0, :] = blocks[:, k, :]
    square = jnp.sum(vector * vector, keepdims=True)
    row, lane = iota((DEV, TILE), 0), iota((DEV, TILE), 1)
    diagonal = jnp.sum(jnp.where(row == lane, gram_r[...], 0.0), axis=1, keepdims=True)
    packed = jnp.where(row > lane, gram_r[...], gram_l[...])
    packed = jnp.where(lane == DIAGONAL, diagonal, packed)
    send[:, PEER_TILES, 0, :] = jnp.where(lane == SQUARE, square, packed)


def tiles_times(sources, tiles, products):
    many = 16
    row = iota((many, TILE), 0)

    for at in range(0, SLOTS, many):
        block = tiles[pl.ds(at, many)].reshape(many * TILE, TILE)
        wide = dot(sources[pl.ds(at, many), :], block, 1, 1)
        total = wide[:, 0:TILE]
        for j in range(1, many):
            total = jnp.where(row == j, wide[:, j * TILE : (j + 1) * TILE], total)
        products[pl.ds(at, many), :] = total


def tiles_times_turned(sources, tiles, products, turned):
    many = 16
    row = iota((many, TILE), 0)
    for at in range(0, SLOTS, many):
        mine = sources[pl.ds(at, many), :]
        blocks = [tiles[at + j].T for j in range(many)]
        for j in range(many):
            turned[at + j] = blocks[j]
        parts = [jnp.where(row == j, mine, jnp.zeros_like(mine)) for j in range(many)]
        block = jnp.concatenate(blocks, axis=0)
        products[pl.ds(at, many), :] = dot(jnp.concatenate(parts, axis=1), block)


def times_tiles(sources, tiles, products):
    many = 16
    row = iota((many, TILE), 0)

    def step(i, carry):
        at = pl.multiple_of(i * many, many)
        block = tiles[pl.ds(at, many)].reshape(many * TILE, TILE)
        mine = sources[pl.ds(at, many), :]
        parts = [jnp.where(row == j, mine, jnp.zeros_like(mine)) for j in range(many)]
        products[pl.ds(at, many), :] = dot(jnp.concatenate(parts, axis=1), block)
        return carry

    lax.fori_loop(0, SLOTS // many, step, 0, unroll=True)


def summed_by_row(row_row, products, out):
    rows = one_hot(iota((GROUP, SLOTS), 0) == row_row[...])
    out[...] = selected(rows, products[...]).reshape(out.shape)


def rows_product_first(
    row_total, arrived, pos_col, row_row, tiles, out, norm, gram_row, turned, sources, products
):
    part = lambda k: arrived[pl.ds(k, DEV, stride=EXTRA), :]
    total = jnp.sum(part(PEER_TILES), axis=0, keepdims=True)
    gram_row[...] = total
    total = jnp.sum(jnp.where(iota((1, TILE), 1) == SQUARE, total, 0.0), axis=1, keepdims=True)
    size = jnp.sqrt(total / row_total + 1e-06)
    norm[...] = jnp.broadcast_to(size, (1, TILE))
    values = jnp.zeros((SLOTS, TILE), F32)
    position = pos_col[...]
    for k in range(PEER_TILES):
        vector = (part(k) / size).astype(BF16)
        hot = one_hot(iota((SLOTS, DEV), 1) * PEER_TILES + k == position)
        values = values + dot(hot, vector)
    sources[...] = values.astype(BF16)
    tiles_times_turned(sources, tiles, products, turned)
    summed_by_row(row_row, products, out)


def rows_product(arrived, pos_col, row_row, tiles, out, sources, products):
    hot = one_hot(iota((SLOTS, NAMED), 1) == pos_col[...])
    vector = arrived[...].reshape(NAMED, TILE)
    sources[...] = dot(hot, vector).astype(BF16)
    times_tiles(sources, tiles, products)
    summed_by_row(row_row, products, out)


def column_product(arrived, row_col, pos_row, tiles, out, sources, products):
    hot = one_hot(iota((SLOTS, GROUP), 1) == row_col[...])
    vector = arrived[...].reshape(GROUP, TILE)
    sources[...] = dot(hot, vector).astype(BF16)
    times_tiles(sources, tiles, products)
    hot = one_hot(iota((NAMED, SLOTS), 0) == pos_row[...])
    out[...] = selected(hot, products[...]).reshape(out.shape)


def image_sums_first(arrived, basis, gram_row, image, out, held):
    vector = jnp.sum(arrived[...], axis=0)
    image[...] = vector
    row = products_row(basis, vector, held)
    out[:, 0, 0:TILE] = jnp.broadcast_to(row, (DEV, TILE))
    out[:, 0, TILE : 2 * TILE] = jnp.broadcast_to(gram_row[...], (DEV, TILE))


def image_sums(arrived, basis, earlier, factor, image, out, held):
    vector = jnp.sum(arrived[...], axis=0) - factor[...] * earlier[...]
    image[...] = vector
    out[:, 0, :] = jnp.broadcast_to(products_row(basis, vector, held), (DEV, TILE))


def back_sums(divide, arrived, basis, place_row, earlier, by, factor, back, out, held):
    hot = one_hot(iota((OWN, NAMED), 0) == place_row[...])
    before = earlier[...] / by[...] if divide else earlier[...]
    vector = selected(hot, arrived[...].reshape(NAMED, TILE)) - factor[...] * before
    back[...] = vector
    out[:, 0, :] = jnp.broadcast_to(products_row(basis, vector, held), (DEV, TILE))


def left_vector_first(row_total, arrived, image, basis, new, copies, norm, gram_r, gram_l):
    got = arrived[:, 0, :]
    both = got[:, TILE : 2 * TILE]
    row, lane = iota((DEV, TILE), 0), iota((DEV, TILE), 1)
    diagonal = jnp.sum(jnp.where(lane == DIAGONAL, both, 0.0), axis=1, keepdims=True)
    gram_r[...] = jnp.where(row > lane, both + both, jnp.where(row == lane, diagonal, 0.0))
    upper = jnp.where(row < lane, both + both, jnp.where(row == lane, both, 0.0))
    gram_l[...] = jnp.where(lane < basis.shape[0], upper, 0.0)
    total = jnp.sum(got[:, 0:TILE], axis=0, keepdims=True)
    finish(row_total, total, image, basis, gram_l, new, norm)
    copies[...] = jnp.broadcast_to(new[...].astype(BF16), copies.shape)


def finish(row_total, total, vector, basis, gram, new, norm):
    size = basis.shape[0]
    projection, square, coeffs, column = coefficients_of(total, size, row_total)
    factor = norm_of(projection, square, coeffs, column, gram, row_total)
    norm[...] = jnp.broadcast_to(factor, (1, TILE))
    subtract_basis(new, vector, basis, column)
    new[...] = new[...] / factor


def left_vector(row_total, arrived, image, basis, gram, new, copies, norm):
    total = jnp.sum(arrived[:, 0, :], axis=0, keepdims=True)
    finish(row_total, total, image, basis, gram, new, norm)
    copies[...] = jnp.broadcast_to(new[...].astype(BF16), copies.shape)


def right_vector(row_total, arrived, back, basis, gram, place_row, new, send, norm):
    total = jnp.sum(arrived[:, 0, :], axis=0, keepdims=True)
    finish(row_total, total, back, basis, gram, new, norm)
    hot = one_hot(iota((OWN, NAMED), 0) == place_row[...])
    blocks = dot(hot, new[...].astype(BF16), 0, 0)
    send[...] = blocks.astype(BF16).reshape(send.shape)


def last_vector(row_total, arrived, back, basis, gram, earlier, left_one, left_two, *rest):
    norms, (left_pair, new_pair, factors, new, norm) = rest[:4], rest[4:]
    left_pair[:, 0, :] = left_one[...]
    left_pair[:, 1, :] = left_two[...]
    total = jnp.sum(arrived[:, 0, :], axis=0, keepdims=True)
    finish(row_total, total, back, basis, gram, new, norm)
    new_pair[:, 0, :] = earlier[...]
    new_pair[:, 1, :] = new[...]
    for i, value in enumerate((*norms, norm)):
        factors[i] = jnp.max(value[...])


VMEM = pl.BlockSpec(memory_space=pltpu.VMEM)
HBM = pl.BlockSpec(memory_space=pltpu.HBM)
SMEM = pl.BlockSpec(memory_space=pltpu.SMEM)


def in_hbm(value):
    return pltpu.with_memory_space_constraint(value, pltpu.HBM)


def call(body, outs, args, scratch=(), in_specs=None, out_specs=None, semaphores=0):
    shapes = [jax.ShapeDtypeStruct(s, d) for s, d in outs]
    return pl.pallas_call(
        body,
        out_shape=shapes,
        in_specs=in_specs or [VMEM] * len(args),
        out_specs=out_specs or [VMEM] * len(outs),
        scratch_shapes=[pltpu.VMEM(s, d) for s, d in scratch]
        + [pltpu.SemaphoreType.DMA((semaphores,))] * (semaphores > 0),
        compiler_params=pltpu.CompilerParams(vmem_limit_bytes=8 << 20),
    )(*(in_hbm(a) if spec is HBM else a for a, spec in zip(args, in_specs or args)))


def to_all(value):
    return lax.all_to_all(value, SEND_ALL, 0, 0, tiled=True)


def in_group(value):
    return lax.all_to_all(value, SEND_COL, 0, 0, tiled=True)


def shards(tiles, row_tiles, col_tiles, counts, right_basis, left_basis, start):
    row_total = float(start.shape[0] * DEV)
    with_total = lambda body: functools.partial(body, row_total)
    own = ((OWN, TILE), F32)
    line = ((1, TILE), F32)
    square = ((DEV, TILE), F32)
    sums = ((DEV, 1, TILE), F32)
    blocks = (DEV, PEER_TILES, TILE)
    in_rows = ((8, OWN, TILE), F32)
    copied = ((8, OWN, TILE), BF16)
    work = [((SLOTS, TILE), BF16), ((SLOTS, TILE), F32)]
    right, left = right_basis, left_basis
    begin = start.reshape(OWN, TILE)
    col_row, row_row = col_tiles.reshape(1, SLOTS), row_tiles.reshape(1, SLOTS)

    pay, rank, col_row, begin, right = call(
        first_sums,
        [sums, ((OWN, DEV), BF16), ((1, SLOTS), I32), own, (right.shape, F32)],
        (col_row, right, begin),
        [square],
        in_specs=[HBM] * 3,
        semaphores=2 + PARTS,
    )
    arrived = to_all(pay)
    pos_row, pos_col, row_row, row_col, gram_r, gram_l = call(
        tables,
        [((1, SLOTS), I32), ((SLOTS, 1), I32)] * 2 + [square, square],
        (counts, rank, col_row, right, row_row, left),
        [(left.shape, F32), ((1, SLOTS), I32)],
        in_specs=[SMEM] + [VMEM] * 3 + [HBM] * 2,
        semaphores=2,
    )
    rest, send, place_row = call(
        with_total(first_vector),
        [own, ((DEV, EXTRA, 1, TILE), F32), ((1, NAMED), I32)],
        (arrived, begin, right, gram_r, gram_l, tiles),
        in_specs=[VMEM] * 5 + [HBM],
    )
    partial, beta_zero, gram_row, turned = call(
        with_total(rows_product_first),
        [in_rows, line, line, (tiles.shape, BF16)],
        (to_all(send).reshape(DEV * EXTRA, TILE), pos_col, row_row, tiles),
        work,
    )
    image, pay = call(
        image_sums_first,
        [own, ((DEV, 1, 2 * TILE), F32)],
        (in_group(partial), left, gram_row),
        [square],
    )
    left_one, copies, alpha_one, gram_r, gram_l = call(
        with_total(left_vector_first),
        [own, copied, line, square, square],
        (to_all(pay), image, left),
    )
    (outgoing,) = call(
        column_product, [(blocks, F32)], (in_group(copies), row_col, pos_row, tiles), work
    )
    back, pay = call(
        functools.partial(back_sums, True),
        [own, sums],
        (to_all(outgoing), right, place_row, rest, beta_zero, alpha_one),
        [square],
    )
    right_two, send, beta_one = call(
        with_total(right_vector),
        [own, (blocks, BF16), line],
        (to_all(pay), back, right, gram_r, place_row),
    )
    (partial,) = call(rows_product, [in_rows], (to_all(send), pos_col, row_row, turned), work)
    image, pay = call(
        image_sums, [own, sums], (in_group(partial), left, left_one, beta_one), [square]
    )
    left_two, copies, alpha_two = call(
        with_total(left_vector), [own, copied, line], (to_all(pay), image, left, gram_l)
    )
    (outgoing,) = call(
        column_product, [(blocks, F32)], (in_group(copies), row_col, pos_row, tiles), work
    )
    back, pay = call(
        functools.partial(back_sums, False),
        [own, sums],
        (to_all(outgoing), right, place_row, right_two, beta_one, alpha_two),
        [square],
    )
    norms = (beta_zero, alpha_one, beta_one, alpha_two)
    lefts, rights, factors = call(
        with_total(last_vector),
        [((OWN, 2, TILE), F32)] * 2 + [((5,), F32)],
        (to_all(pay), back, right, gram_r, right_two, left_one, left_two, *norms),
        [own, line],
        out_specs=[VMEM, VMEM, SMEM],
    )
    as_rows = lambda pair: pair.transpose(1, 0, 2).reshape(2, OWN * TILE)
    return as_rows(lefts), as_rows(rights), factors


def solution(mesh):
    torus = Mesh(mesh.devices.reshape(4, 4, 4, 2), ALL)
    placed = (
        P(ALL, None, None),
        P(ALL),
        P(ALL),
        P(ALL),
        P(None, ALL),
        P(None, ALL),
        P(ALL),
    )
    return jax.shard_map(
        shards,
        mesh=torus,
        in_specs=placed,
        out_specs=(P(None, ALL), P(None, ALL), P()),
        check_vma=False,
    )
```

```python
import functools

import jax
import jax.numpy as jnp
from jax import lax
from jax.experimental import pallas as pl
from jax.experimental.pallas import tpu as pltpu
from jax.sharding import Mesh
from jax.sharding import PartitionSpec as P

PEER_TILES = 8
ALL = ("row_0", "row_1", "col_0", "col_1")
SEND_ALL = ("col_1", "col_0", "row_1", "row_0")
SEND_COL = ("col_1", "col_0")
HIGH = lax.Precision.HIGHEST
F32, BF16, I32 = jnp.float32, jnp.bfloat16, jnp.int32

DEV = 128
OWN = 32
TILE = 128
SLOTS = 512
GROUP = 256
NAMED = DEV * PEER_TILES
PLACE = 104
PARTS = 4
SQUARE, DIAGONAL = 126, 127
EXTRA = PEER_TILES + 1


def iota(shape, dim):
    return lax.broadcasted_iota(I32, shape, dim)


def block_of(device):
    near = (device % 2) * 64 + (device // 2 % 4) * 16
    return near + (device // 8 % 4) * 4 + device // 32


def group_row_of(row):
    owner = row // OWN
    return ((owner % 2) * 4 + owner // 2) * OWN + row % OWN


def one_hot(condition):
    return jnp.where(condition, 1.0, 0.0).astype(BF16)


def dot(a, b, ca=1, cb=0, precision=None):
    return lax.dot_general(
        a, b, (((ca,), (cb,)), ((), ())), precision=precision, preferred_element_type=F32
    )


def selected(hot, value):
    first = value.astype(BF16)
    rest = value - first.astype(F32)
    second = rest.astype(BF16)
    third = (rest - second.astype(F32)).astype(BF16)
    return dot(hot, third) + dot(hot, second) + dot(hot, first)


def products_row(basis, vector, held, copies=()):
    size = basis.shape[0]
    total = jnp.zeros((size, TILE), F32)
    for k in range(OWN):
        if copies and k % (OWN // PARTS) == 0:
            copies[k // (OWN // PARTS)].wait()
        total = total + basis[:, k * TILE : (k + 1) * TILE] * vector[k : k + 1, :]
    held[...] = jnp.zeros_like(held)
    held[0:size, :] = total
    row = jnp.sum(held[...].T, axis=0, keepdims=True)
    square = jnp.sum(vector * vector, keepdims=True)
    return jnp.where(iota((1, TILE), 1) == size, square, row)


def coefficients_of(total, size, row_total):
    lane = iota((1, TILE), 1)
    projection = jnp.where(lane < size, total, 0.0)
    square = jnp.sum(jnp.where(lane == size, total, 0.0), axis=1, keepdims=True)
    coeffs = projection / row_total
    diagonal = iota((size, TILE), 0) == iota((size, TILE), 1)
    column = jnp.sum(jnp.where(diagonal, coeffs, 0.0), axis=1, keepdims=True)
    return projection, square, coeffs, column


def subtract_basis(out, vector, basis, column):
    wide = jnp.broadcast_to(column, (column.shape[0], TILE))
    for k in range(OWN):
        part = jnp.sum(basis[:, k * TILE : (k + 1) * TILE] * wide, axis=0, keepdims=True)
        out[k : k + 1, :] = vector[k : k + 1, :] - part


def norm_of(projection, square, coeffs, column, gram, row_total):
    size = column.shape[0]
    applied = jnp.sum(gram[0:size, :] * coeffs, axis=1, keepdims=True)
    quadratic = jnp.sum(applied * column, axis=0, keepdims=True)
    linear = jnp.sum(coeffs * projection, axis=1, keepdims=True)
    left = jnp.maximum(square - 2.0 * linear + quadratic, 0.0)
    return jnp.sqrt(left / row_total + 1e-06)


def first_sums(col_hbm, basis_hbm, start_hbm, out, rank, col_row, start, basis, held, sems):
    wide = basis.shape[1] // PARTS
    parts = [pl.ds(i * wide, wide) for i in range(PARTS)]
    copies = [pltpu.make_async_copy(col_hbm, col_row, sems.at[0])]
    copies += [pltpu.make_async_copy(start_hbm, start, sems.at[1])]
    copies += [
        pltpu.make_async_copy(basis_hbm.at[:, part], basis.at[:, part], sems.at[2 + i])
        for i, part in enumerate(parts)
    ]
    for copy in copies:
        copy.start()
    copies[0].wait()
    owner, place = block_of(col_row[...] // OWN), col_row[...] % OWN
    owners = one_hot(iota((DEV, SLOTS), 0) == owner)
    places = one_hot(iota((OWN, SLOTS), 0) == place)
    touched = dot(places, owners, 1, 1) > 0.5
    below = one_hot(iota((OWN, OWN), 1) < iota((OWN, OWN), 0))
    places = dot(below, one_hot(touched))
    rank[...] = places.astype(BF16)
    copies[1].wait()
    row = products_row(basis, start[...], held, copies[2:])
    held[...] = jnp.zeros_like(held)
    number = (iota((OWN, DEV), 0) + 1).astype(F32)
    for k in range(PEER_TILES):
        here = touched & (places > k - 0.5) & (places < k + 0.5)
        named = jnp.sum(jnp.where(here, number, 0.0), axis=0, keepdims=True)
        held[PLACE + k : PLACE + k + 1, :] = named - 1.0
    out[:, 0, :] = held[...].T + row


def gram_of(basis):
    value = basis[...]
    first = value.astype(BF16)
    rest = value - first.astype(F32)
    second = rest.astype(BF16)
    third = (rest - second.astype(F32)).astype(BF16)
    low = dot(third, first, 1, 1)
    middle = dot(second, first, 1, 1)
    both = low + middle
    return dot(second, second, 1, 1) + (both + both.T) + dot(first, first, 1, 1)


def tables(counts, rank, col_row, right, row_hbm, left_hbm, *refs):
    pos_row, pos_col, row_row, row_col, gram_r, gram_l, left, given_row, sems = refs
    wide = left.shape[1] // PARTS
    parts = [pl.ds(i * wide, wide) for i in range(PARTS)]
    copies = [pltpu.make_async_copy(row_hbm, given_row, sems.at[PARTS])]
    copies += [
        pltpu.make_async_copy(left_hbm.at[:, part], left.at[:, part], sems.at[i])
        for i, part in enumerate(parts)
    ]
    for copy in copies:
        copy.start()
    gram_r[...] = jnp.zeros_like(gram_r)
    gram_l[...] = jnp.zeros_like(gram_l)
    size = right.shape[0]
    gram_r[0:size, 0:size] = gram_of(right)
    copies[0].wait()
    row = group_row_of(given_row[...])
    row_row[...] = row
    count = counts[...]
    owner, place = block_of(col_row[...] // OWN), col_row[...] % OWN
    owners = one_hot(iota((DEV, SLOTS), 0) == owner)
    mine = dot(rank[...], owners)
    mine = jnp.where(iota((OWN, SLOTS), 0) == place, mine, 0.0)
    position = owner * PEER_TILES + jnp.sum(mine, axis=0, keepdims=True).astype(I32)
    position = jnp.where(iota((1, SLOTS), 1) < count, position, -1)
    pos_row[...] = position
    both = jnp.where(iota((8, SLOTS), 0) == 0, position, row)
    columns = both.astype(F32).T.astype(I32)
    pos_col[...] = columns[:, 0:1]
    row_col[...] = columns[:, 1:2]
    for copy in copies[1:]:
        copy.wait()
    gram_l[0:size, 0:size] = gram_of(left)


def place_row_of(arrived):
    lane = iota((DEV, NAMED), 0)
    spread = dot(arrived.astype(BF16), one_hot(lane - PLACE == iota((DEV, NAMED), 1) % PEER_TILES))
    own = iota((DEV, NAMED), 1) // PEER_TILES == lane
    row = jnp.sum(jnp.where(own, spread, 0.0), axis=0, keepdims=True)
    return jnp.round(row).astype(I32)


def first_vector(row_total, arrived, start, basis, gram_r, gram_l, _, rest, send, place_row):
    size = basis.shape[0]
    got = arrived[:, 0, :]
    total = jnp.sum(got, axis=0, keepdims=True)
    _, _, _, column = coefficients_of(total, size, row_total)
    named = place_row_of(got)
    place_row[...] = named
    subtract_basis(rest, start, basis, column)
    vector = rest[...]
    hot = jnp.where(iota((OWN, NAMED), 0) == named, 1.0, 0.0)
    blocks = dot(hot, vector, 0, 0, HIGH).reshape(DEV, PEER_TILES, TILE)
    for k in range(PEER_TILES):
        send[:, k, 0, :] = blocks[:, k, :]
    square = jnp.sum(vector * vector, keepdims=True)
    row, lane = iota((DEV, TILE), 0), iota((DEV, TILE), 1)
    diagonal = jnp.sum(jnp.where(row == lane, gram_r[...], 0.0), axis=1, keepdims=True)
    packed = jnp.where(row > lane, gram_r[...], gram_l[...])
    packed = jnp.where(lane == DIAGONAL, diagonal, packed)
    send[:, PEER_TILES, 0, :] = jnp.where(lane == SQUARE, square, packed)


def tiles_times(sources, tiles, products):
    many = 16
    row = iota((many, TILE), 0)

    for at in range(0, SLOTS, many):
        block = tiles[pl.ds(at, many)].reshape(many * TILE, TILE)
        wide = dot(sources[pl.ds(at, many), :], block, 1, 1)
        total = wide[:, 0:TILE]
        for j in range(1, many):
            total = jnp.where(row == j, wide[:, j * TILE : (j + 1) * TILE], total)
        products[pl.ds(at, many), :] = total


def tiles_times_turned(sources, tiles, products, turned):
    many = 16
    row = iota((many, TILE), 0)
    for at in range(0, SLOTS, many):
        mine = sources[pl.ds(at, many), :]
        blocks = [tiles[at + j].T for j in range(many)]
        for j in range(many):
            turned[at + j] = blocks[j]
        parts = [jnp.where(row == j, mine, jnp.zeros_like(mine)) for j in range(many)]
        block = jnp.concatenate(blocks, axis=0)
        products[pl.ds(at, many), :] = dot(jnp.concatenate(parts, axis=1), block)


def times_tiles(sources, tiles, products):
    many = 16
    row = iota((many, TILE), 0)

    def step(i, carry):
        at = pl.multiple_of(i * many, many)
        block = tiles[pl.ds(at, many)].reshape(many * TILE, TILE)
        mine = sources[pl.ds(at, many), :]
        parts = [jnp.where(row == j, mine, jnp.zeros_like(mine)) for j in range(many)]
        products[pl.ds(at, many), :] = dot(jnp.concatenate(parts, axis=1), block)
        return carry

    lax.fori_loop(0, SLOTS // many, step, 0, unroll=True)


def summed_by_row(row_row, products, out):
    rows = one_hot(iota((GROUP, SLOTS), 0) == row_row[...])
    out[...] = selected(rows, products[...]).reshape(out.shape)


def rows_product_first(
    row_total, arrived, pos_col, row_row, tiles, out, norm, gram_row, turned, sources, products
):
    part = lambda k: arrived[pl.ds(k, DEV, stride=EXTRA), :]
    total = jnp.sum(part(PEER_TILES), axis=0, keepdims=True)
    gram_row[...] = total
    total = jnp.sum(jnp.where(iota((1, TILE), 1) == SQUARE, total, 0.0), axis=1, keepdims=True)
    size = jnp.sqrt(total / row_total + 1e-06)
    norm[...] = jnp.broadcast_to(size, (1, TILE))
    values = jnp.zeros((SLOTS, TILE), F32)
    position = pos_col[...]
    for k in range(PEER_TILES):
        vector = (part(k) / size).astype(BF16)
        hot = one_hot(iota((SLOTS, DEV), 1) * PEER_TILES + k == position)
        values = values + dot(hot, vector)
    sources[...] = values.astype(BF16)
    tiles_times_turned(sources, tiles, products, turned)
    summed_by_row(row_row, products, out)


def rows_product(arrived, pos_col, row_row, tiles, out, sources, products):
    hot = one_hot(iota((SLOTS, NAMED), 1) == pos_col[...])
    vector = arrived[...].reshape(NAMED, TILE)
    sources[...] = dot(hot, vector).astype(BF16)
    times_tiles(sources, tiles, products)
    summed_by_row(row_row, products, out)


def column_product(arrived, row_col, pos_row, tiles, out, sources, products):
    hot = one_hot(iota((SLOTS, GROUP), 1) == row_col[...])
    vector = arrived[...].reshape(GROUP, TILE)
    sources[...] = dot(hot, vector).astype(BF16)
    times_tiles(sources, tiles, products)
    hot = one_hot(iota((NAMED, SLOTS), 0) == pos_row[...])
    out[...] = selected(hot, products[...]).reshape(out.shape)


def image_sums_first(arrived, basis, gram_row, image, out, held):
    vector = jnp.sum(arrived[...], axis=0)
    image[...] = vector
    row = products_row(basis, vector, held)
    out[:, 0, 0:TILE] = jnp.broadcast_to(row, (DEV, TILE))
    out[:, 0, TILE : 2 * TILE] = jnp.broadcast_to(gram_row[...], (DEV, TILE))


def image_sums(arrived, basis, earlier, factor, image, out, held):
    vector = jnp.sum(arrived[...], axis=0) - factor[...] * earlier[...]
    image[...] = vector
    out[:, 0, :] = jnp.broadcast_to(products_row(basis, vector, held), (DEV, TILE))


def back_sums(divide, arrived, basis, place_row, earlier, by, factor, back, out, held):
    hot = one_hot(iota((OWN, NAMED), 0) == place_row[...])
    before = earlier[...] / by[...] if divide else earlier[...]
    vector = selected(hot, arrived[...].reshape(NAMED, TILE)) - factor[...] * before
    back[...] = vector
    out[:, 0, :] = jnp.broadcast_to(products_row(basis, vector, held), (DEV, TILE))


def left_vector_first(row_total, arrived, image, basis, new, copies, norm, gram_r, gram_l):
    got = arrived[:, 0, :]
    both = got[:, TILE : 2 * TILE]
    row, lane = iota((DEV, TILE), 0), iota((DEV, TILE), 1)
    diagonal = jnp.sum(jnp.where(lane == DIAGONAL, both, 0.0), axis=1, keepdims=True)
    gram_r[...] = jnp.where(row > lane, both + both, jnp.where(row == lane, diagonal, 0.0))
    upper = jnp.where(row < lane, both + both, jnp.where(row == lane, both, 0.0))
    gram_l[...] = jnp.where(lane < basis.shape[0], upper, 0.0)
    total = jnp.sum(got[:, 0:TILE], axis=0, keepdims=True)
    finish(row_total, total, image, basis, gram_l, new, norm)
    copies[...] = jnp.broadcast_to(new[...].astype(BF16), copies.shape)


def finish(row_total, total, vector, basis, gram, new, norm):
    size = basis.shape[0]
    projection, square, coeffs, column = coefficients_of(total, size, row_total)
    factor = norm_of(projection, square, coeffs, column, gram, row_total)
    norm[...] = jnp.broadcast_to(factor, (1, TILE))
    subtract_basis(new, vector, basis, column)
    new[...] = new[...] / factor


def left_vector(row_total, arrived, image, basis, gram, new, copies, norm):
    total = jnp.sum(arrived[:, 0, :], axis=0, keepdims=True)
    finish(row_total, total, image, basis, gram, new, norm)
    copies[...] = jnp.broadcast_to(new[...].astype(BF16), copies.shape)


def right_vector(row_total, arrived, back, basis, gram, place_row, new, send, norm):
    total = jnp.sum(arrived[:, 0, :], axis=0, keepdims=True)
    finish(row_total, total, back, basis, gram, new, norm)
    hot = one_hot(iota((OWN, NAMED), 0) == place_row[...])
    blocks = dot(hot, new[...].astype(BF16), 0, 0)
    send[...] = blocks.astype(BF16).reshape(send.shape)


def last_vector(row_total, arrived, back, basis, gram, earlier, left_one, left_two, *rest):
    norms, (left_pair, new_pair, factors, new, norm) = rest[:4], rest[4:]
    left_pair[:, 0, :] = left_one[...]
    left_pair[:, 1, :] = left_two[...]
    total = jnp.sum(arrived[:, 0, :], axis=0, keepdims=True)
    finish(row_total, total, back, basis, gram, new, norm)
    new_pair[:, 0, :] = earlier[...]
    new_pair[:, 1, :] = new[...]
    for i, value in enumerate((*norms, norm)):
        factors[i] = jnp.max(value[...])


VMEM = pl.BlockSpec(memory_space=pltpu.VMEM)
HBM = pl.BlockSpec(memory_space=pltpu.HBM)
SMEM = pl.BlockSpec(memory_space=pltpu.SMEM)


def in_hbm(value):
    return pltpu.with_memory_space_constraint(value, pltpu.HBM)


def call(body, outs, args, scratch=(), in_specs=None, out_specs=None, semaphores=0):
    shapes = [jax.ShapeDtypeStruct(s, d) for s, d in outs]
    return pl.pallas_call(
        body,
        out_shape=shapes,
        in_specs=in_specs or [VMEM] * len(args),
        out_specs=out_specs or [VMEM] * len(outs),
        scratch_shapes=[pltpu.VMEM(s, d) for s, d in scratch]
        + [pltpu.SemaphoreType.DMA((semaphores,))] * (semaphores > 0),
        compiler_params=pltpu.CompilerParams(vmem_limit_bytes=8 << 20),
    )(*(in_hbm(a) if spec is HBM else a for a, spec in zip(args, in_specs or args)))


def to_all(value):
    return lax.all_to_all(value, SEND_ALL, 0, 0, tiled=True)


def in_group(value):
    return lax.all_to_all(value, SEND_COL, 0, 0, tiled=True)


def shards(tiles, row_tiles, col_tiles, counts, right_basis, left_basis, start):
    row_total = float(start.shape[0] * DEV)
    with_total = lambda body: functools.partial(body, row_total)
    own = ((OWN, TILE), F32)
    line = ((1, TILE), F32)
    square = ((DEV, TILE), F32)
    sums = ((DEV, 1, TILE), F32)
    blocks = (DEV, PEER_TILES, TILE)
    in_rows = ((8, OWN, TILE), F32)
    copied = ((8, OWN, TILE), BF16)
    work = [((SLOTS, TILE), BF16), ((SLOTS, TILE), F32)]
    right, left = right_basis, left_basis
    begin = start.reshape(OWN, TILE)
    col_row, row_row = col_tiles.reshape(1, SLOTS), row_tiles.reshape(1, SLOTS)

    pay, rank, col_row, begin, right = call(
        first_sums,
        [sums, ((OWN, DEV), BF16), ((1, SLOTS), I32), own, (right.shape, F32)],
        (col_row, right, begin),
        [square],
        in_specs=[HBM] * 3,
        semaphores=2 + PARTS,
    )
    arrived = to_all(pay)
    pos_row, pos_col, row_row, row_col, gram_r, gram_l = call(
        tables,
        [((1, SLOTS), I32), ((SLOTS, 1), I32)] * 2 + [square, square],
        (counts.reshape(1, 1), rank, col_row, right, row_row, left),
        [(left.shape, F32), ((1, SLOTS), I32)],
        in_specs=[VMEM] * 4 + [HBM] * 2,
        semaphores=PARTS + 1,
    )
    rest, send, place_row = call(
        with_total(first_vector),
        [own, ((DEV, EXTRA, 1, TILE), F32), ((1, NAMED), I32)],
        (arrived, begin, right, gram_r, gram_l, tiles),
        in_specs=[VMEM] * 5 + [HBM],
    )
    partial, beta_zero, gram_row, turned = call(
        with_total(rows_product_first),
        [in_rows, line, line, (tiles.shape, BF16)],
        (to_all(send).reshape(DEV * EXTRA, TILE), pos_col, row_row, tiles),
        work,
    )
    image, pay = call(
        image_sums_first,
        [own, ((DEV, 1, 2 * TILE), F32)],
        (in_group(partial), left, gram_row),
        [square],
    )
    left_one, copies, alpha_one, gram_r, gram_l = call(
        with_total(left_vector_first),
        [own, copied, line, square, square],
        (to_all(pay), image, left),
    )
    (outgoing,) = call(
        column_product, [(blocks, F32)], (in_group(copies), row_col, pos_row, tiles), work
    )
    back, pay = call(
        functools.partial(back_sums, True),
        [own, sums],
        (to_all(outgoing), right, place_row, rest, beta_zero, alpha_one),
        [square],
    )
    right_two, send, beta_one = call(
        with_total(right_vector),
        [own, (blocks, BF16), line],
        (to_all(pay), back, right, gram_r, place_row),
    )
    (partial,) = call(rows_product, [in_rows], (to_all(send), pos_col, row_row, turned), work)
    image, pay = call(
        image_sums, [own, sums], (in_group(partial), left, left_one, beta_one), [square]
    )
    left_two, copies, alpha_two = call(
        with_total(left_vector), [own, copied, line], (to_all(pay), image, left, gram_l)
    )
    (outgoing,) = call(
        column_product, [(blocks, F32)], (in_group(copies), row_col, pos_row, tiles), work
    )
    back, pay = call(
        functools.partial(back_sums, False),
        [own, sums],
        (to_all(outgoing), right, place_row, right_two, beta_one, alpha_two),
        [square],
    )
    norms = (beta_zero, alpha_one, beta_one, alpha_two)
    lefts, rights, factors = call(
        with_total(last_vector),
        [((OWN, 2, TILE), F32)] * 2 + [((5,), F32)],
        (to_all(pay), back, right, gram_r, right_two, left_one, left_two, *norms),
        [own, line],
        out_specs=[VMEM, VMEM, SMEM],
    )
    as_rows = lambda pair: pair.transpose(1, 0, 2).reshape(2, OWN * TILE)
    return as_rows(lefts), as_rows(rights), factors


def solution(mesh):
    torus = Mesh(mesh.devices.reshape(4, 4, 4, 2), ALL)
    placed = (
        P(ALL, None, None),
        P(ALL),
        P(ALL),
        P(ALL),
        P(None, ALL),
        P(None, ALL),
        P(ALL),
    )
    return jax.shard_map(
        shards,
        mesh=torus,
        in_specs=placed,
        out_specs=(P(None, ALL), P(None, ALL), P()),
        check_vma=False,
    )
```

```python
import functools

import jax
import jax.numpy as jnp
from jax import lax
from jax.experimental import pallas as pl
from jax.experimental.pallas import tpu as pltpu
from jax.sharding import Mesh
from jax.sharding import PartitionSpec as P

PEER_TILES = 8
ALL = ("row_0", "row_1", "col_0", "col_1")
SEND_ALL = ("col_1", "col_0", "row_1", "row_0")
SEND_COL = ("col_1", "col_0")
HIGH = lax.Precision.HIGHEST
F32, BF16, I32 = jnp.float32, jnp.bfloat16, jnp.int32

DEV = 128
OWN = 32
TILE = 128
SLOTS = 512
GROUP = 256
NAMED = DEV * PEER_TILES
PLACE = 104
PARTS = 4
SQUARE, DIAGONAL = 126, 127
EXTRA = PEER_TILES + 1


def iota(shape, dim):
    return lax.broadcasted_iota(I32, shape, dim)


def block_of(device):
    near = (device % 2) * 64 + (device // 2 % 4) * 16
    return near + (device // 8 % 4) * 4 + device // 32


def group_row_of(row):
    owner = row // OWN
    return ((owner % 2) * 4 + owner // 2) * OWN + row % OWN


def one_hot(condition):
    return jnp.where(condition, 1.0, 0.0).astype(BF16)


def dot(a, b, ca=1, cb=0, precision=None):
    return lax.dot_general(
        a, b, (((ca,), (cb,)), ((), ())), precision=precision, preferred_element_type=F32
    )


def selected(hot, value):
    first = value.astype(BF16)
    rest = value - first.astype(F32)
    second = rest.astype(BF16)
    third = (rest - second.astype(F32)).astype(BF16)
    return dot(hot, third) + dot(hot, second) + dot(hot, first)


def products_row(basis, vector, held, copies=()):
    size = basis.shape[0]
    total = jnp.zeros((size, TILE), F32)
    for k in range(OWN):
        if copies and k % (OWN // PARTS) == 0:
            copies[k // (OWN // PARTS)].wait()
        total = total + basis[:, k * TILE : (k + 1) * TILE] * vector[k : k + 1, :]
    held[...] = jnp.zeros_like(held)
    held[0:size, :] = total
    row = jnp.sum(held[...].T, axis=0, keepdims=True)
    square = jnp.sum(vector * vector, keepdims=True)
    return jnp.where(iota((1, TILE), 1) == size, square, row)


def coefficients_of(total, size, row_total):
    lane = iota((1, TILE), 1)
    projection = jnp.where(lane < size, total, 0.0)
    square = jnp.sum(jnp.where(lane == size, total, 0.0), axis=1, keepdims=True)
    coeffs = projection / row_total
    diagonal = iota((size, TILE), 0) == iota((size, TILE), 1)
    column = jnp.sum(jnp.where(diagonal, coeffs, 0.0), axis=1, keepdims=True)
    return projection, square, coeffs, column


def subtract_basis(out, vector, basis, column):
    wide = jnp.broadcast_to(column, (column.shape[0], TILE))
    for k in range(OWN):
        part = jnp.sum(basis[:, k * TILE : (k + 1) * TILE] * wide, axis=0, keepdims=True)
        out[k : k + 1, :] = vector[k : k + 1, :] - part


def norm_of(projection, square, coeffs, column, gram, row_total):
    size = column.shape[0]
    applied = jnp.sum(gram[0:size, :] * coeffs, axis=1, keepdims=True)
    quadratic = jnp.sum(applied * column, axis=0, keepdims=True)
    linear = jnp.sum(coeffs * projection, axis=1, keepdims=True)
    left = jnp.maximum(square - 2.0 * linear + quadratic, 0.0)
    return jnp.sqrt(left / row_total + 1e-06)


def first_sums(col_hbm, row_hbm, basis_hbm, start_hbm, out, pos_row, pos_col, row_row, *refs):
    row_col, start, basis, held, listed, col_row, given_row, sems = refs
    wide = basis.shape[1] // PARTS
    parts = [pl.ds(i * wide, wide) for i in range(PARTS)]
    copies = [
        pltpu.make_async_copy(col_hbm, col_row, sems.at[0]),
        pltpu.make_async_copy(row_hbm, given_row, sems.at[1]),
        pltpu.make_async_copy(start_hbm, start, sems.at[2]),
    ]
    copies += [
        pltpu.make_async_copy(basis_hbm.at[:, part], basis.at[:, part], sems.at[3 + i])
        for i, part in enumerate(parts)
    ]
    for copy in copies:
        copy.start()
    copies[0].wait()
    owner, place = block_of(col_row[...] // OWN), col_row[...] % OWN
    owners = one_hot(iota((DEV, SLOTS), 0) == owner)
    in_place = iota((OWN, SLOTS), 0) == place
    touched = dot(one_hot(in_place), owners, 1, 1) > 0.5
    below = one_hot(iota((OWN, OWN), 1) < iota((OWN, OWN), 0))
    rank = dot(below, one_hot(touched))
    listed[...] = jnp.zeros_like(listed)
    number = (iota((OWN, DEV), 0) + 1).astype(F32)
    for k in range(PEER_TILES):
        here = touched & (rank > k - 0.5) & (rank < k + 0.5)
        named = jnp.sum(jnp.where(here, number, 0.0), axis=0, keepdims=True)
        listed[PLACE + k : PLACE + k + 1, :] = named - 1.0
    places = listed[...].T
    mine = jnp.where(in_place, dot(rank.astype(BF16), owners), 0.0)
    position = owner * PEER_TILES + jnp.sum(mine, axis=0, keepdims=True).astype(I32)
    pos_row[...] = position
    copies[1].wait()
    row = group_row_of(given_row[...])
    row_row[...] = row
    both = jnp.where(iota((8, SLOTS), 0) == 0, position, row)
    columns = both.astype(F32).T.astype(I32)
    pos_col[...] = columns[:, 0:1]
    row_col[...] = columns[:, 1:2]
    copies[2].wait()
    out[:, 0, :] = places + products_row(basis, start[...], held, copies[3:])


def gram_of(basis):
    value = basis[...]
    first = value.astype(BF16)
    rest = value - first.astype(F32)
    second = rest.astype(BF16)
    third = (rest - second.astype(F32)).astype(BF16)
    low = dot(third, first, 1, 1)
    middle = dot(second, first, 1, 1)
    both = low + middle
    return dot(second, second, 1, 1) + (both + both.T) + dot(first, first, 1, 1)


def tables(counts, all_row, all_col, right, left_hbm, pos_row, pos_col, gram_r, gram_l, left, sems):
    copy = pltpu.make_async_copy(left_hbm, left, sems.at[0])
    copy.start()
    size = right.shape[0]
    gram_r[...] = jnp.zeros_like(gram_r)
    gram_l[...] = jnp.zeros_like(gram_l)
    gram_r[0:size, 0:size] = gram_of(right)
    copy.wait()
    gram_l[0:size, 0:size] = gram_of(left)
    pos_row[...] = jnp.where(iota((1, SLOTS), 1) < counts[...], all_row[...], -1)
    pos_col[...] = jnp.where(iota((SLOTS, 1), 0) < counts[...], all_col[...], -1)


def place_row_of(arrived):
    lane = iota((DEV, NAMED), 0)
    spread = dot(arrived.astype(BF16), one_hot(lane - PLACE == iota((DEV, NAMED), 1) % PEER_TILES))
    own = iota((DEV, NAMED), 1) // PEER_TILES == lane
    row = jnp.sum(jnp.where(own, spread, 0.0), axis=0, keepdims=True)
    return jnp.round(row).astype(I32)


def first_vector(row_total, arrived, start, basis, gram_r, gram_l, _, rest, send, place_row):
    size = basis.shape[0]
    got = arrived[:, 0, :]
    total = jnp.sum(got, axis=0, keepdims=True)
    _, _, _, column = coefficients_of(total, size, row_total)
    named = place_row_of(got)
    place_row[...] = named
    subtract_basis(rest, start, basis, column)
    vector = rest[...]
    hot = jnp.where(iota((OWN, NAMED), 0) == named, 1.0, 0.0)
    blocks = dot(hot, vector, 0, 0, HIGH).reshape(DEV, PEER_TILES, TILE)
    for k in range(PEER_TILES):
        send[:, k, 0, :] = blocks[:, k, :]
    square = jnp.sum(vector * vector, keepdims=True)
    row, lane = iota((DEV, TILE), 0), iota((DEV, TILE), 1)
    diagonal = jnp.sum(jnp.where(row == lane, gram_r[...], 0.0), axis=1, keepdims=True)
    packed = jnp.where(row > lane, gram_r[...], gram_l[...])
    packed = jnp.where(lane == DIAGONAL, diagonal, packed)
    send[:, PEER_TILES, 0, :] = jnp.where(lane == SQUARE, square, packed)


def tiles_times(sources, tiles, products):
    many = 16
    row = iota((many, TILE), 0)

    for at in range(0, SLOTS, many):
        block = tiles[pl.ds(at, many)].reshape(many * TILE, TILE)
        wide = dot(sources[pl.ds(at, many), :], block, 1, 1)
        total = wide[:, 0:TILE]
        for j in range(1, many):
            total = jnp.where(row == j, wide[:, j * TILE : (j + 1) * TILE], total)
        products[pl.ds(at, many), :] = total


def tiles_times_turned(sources, tiles, products, turned):
    many = 16
    row = iota((many, TILE), 0)
    for at in range(0, SLOTS, many):
        mine = sources[pl.ds(at, many), :]
        blocks = [tiles[at + j].T for j in range(many)]
        for j in range(many):
            turned[at + j] = blocks[j]
        parts = [jnp.where(row == j, mine, jnp.zeros_like(mine)) for j in range(many)]
        block = jnp.concatenate(blocks, axis=0)
        products[pl.ds(at, many), :] = dot(jnp.concatenate(parts, axis=1), block)


def times_tiles(sources, tiles, products):
    many = 16
    row = iota((many, TILE), 0)

    def step(i, carry):
        at = pl.multiple_of(i * many, many)
        block = tiles[pl.ds(at, many)].reshape(many * TILE, TILE)
        mine = sources[pl.ds(at, many), :]
        parts = [jnp.where(row == j, mine, jnp.zeros_like(mine)) for j in range(many)]
        products[pl.ds(at, many), :] = dot(jnp.concatenate(parts, axis=1), block)
        return carry

    lax.fori_loop(0, SLOTS // many, step, 0, unroll=True)


def summed_by_row(row_row, products, out):
    rows = one_hot(iota((GROUP, SLOTS), 0) == row_row[...])
    out[...] = selected(rows, products[...]).reshape(out.shape)


def rows_product_first(
    row_total, arrived, pos_col, row_row, tiles, out, norm, gram_row, turned, sources, products
):
    part = lambda k: arrived[pl.ds(k, DEV, stride=EXTRA), :]
    total = jnp.sum(part(PEER_TILES), axis=0, keepdims=True)
    gram_row[...] = total
    total = jnp.sum(jnp.where(iota((1, TILE), 1) == SQUARE, total, 0.0), axis=1, keepdims=True)
    size = jnp.sqrt(total / row_total + 1e-06)
    norm[...] = jnp.broadcast_to(size, (1, TILE))
    values = jnp.zeros((SLOTS, TILE), F32)
    position = pos_col[...]
    for k in range(PEER_TILES):
        vector = (part(k) / size).astype(BF16)
        hot = one_hot(iota((SLOTS, DEV), 1) * PEER_TILES + k == position)
        values = values + dot(hot, vector)
    sources[...] = values.astype(BF16)
    tiles_times_turned(sources, tiles, products, turned)
    summed_by_row(row_row, products, out)


def rows_product(arrived, pos_col, row_row, tiles, out, sources, products):
    hot = one_hot(iota((SLOTS, NAMED), 1) == pos_col[...])
    vector = arrived[...].reshape(NAMED, TILE)
    sources[...] = dot(hot, vector).astype(BF16)
    times_tiles(sources, tiles, products)
    summed_by_row(row_row, products, out)


def column_product(arrived, row_col, pos_row, tiles, out, sources, products):
    hot = one_hot(iota((SLOTS, GROUP), 1) == row_col[...])
    vector = arrived[...].reshape(GROUP, TILE)
    sources[...] = dot(hot, vector).astype(BF16)
    times_tiles(sources, tiles, products)
    hot = one_hot(iota((NAMED, SLOTS), 0) == pos_row[...])
    out[...] = selected(hot, products[...]).reshape(out.shape)


def image_sums_first(arrived, basis, gram_row, image, out, held):
    vector = jnp.sum(arrived[...], axis=0)
    image[...] = vector
    row = products_row(basis, vector, held)
    out[:, 0, 0:TILE] = jnp.broadcast_to(row, (DEV, TILE))
    out[:, 0, TILE : 2 * TILE] = jnp.broadcast_to(gram_row[...], (DEV, TILE))


def image_sums(arrived, basis, earlier, factor, image, out, held):
    vector = jnp.sum(arrived[...], axis=0) - factor[...] * earlier[...]
    image[...] = vector
    out[:, 0, :] = jnp.broadcast_to(products_row(basis, vector, held), (DEV, TILE))


def back_sums(divide, arrived, basis, place_row, earlier, by, factor, back, out, held):
    hot = one_hot(iota((OWN, NAMED), 0) == place_row[...])
    before = earlier[...] / by[...] if divide else earlier[...]
    vector = selected(hot, arrived[...].reshape(NAMED, TILE)) - factor[...] * before
    back[...] = vector
    out[:, 0, :] = jnp.broadcast_to(products_row(basis, vector, held), (DEV, TILE))


def left_vector_first(row_total, arrived, image, basis, new, copies, norm, gram_r, gram_l):
    got = arrived[:, 0, :]
    both = got[:, TILE : 2 * TILE]
    row, lane = iota((DEV, TILE), 0), iota((DEV, TILE), 1)
    diagonal = jnp.sum(jnp.where(lane == DIAGONAL, both, 0.0), axis=1, keepdims=True)
    gram_r[...] = jnp.where(row > lane, both + both, jnp.where(row == lane, diagonal, 0.0))
    upper = jnp.where(row < lane, both + both, jnp.where(row == lane, both, 0.0))
    gram_l[...] = jnp.where(lane < basis.shape[0], upper, 0.0)
    total = jnp.sum(got[:, 0:TILE], axis=0, keepdims=True)
    finish(row_total, total, image, basis, gram_l, new, norm)
    copies[...] = jnp.broadcast_to(new[...].astype(BF16), copies.shape)


def finish(row_total, total, vector, basis, gram, new, norm):
    size = basis.shape[0]
    projection, square, coeffs, column = coefficients_of(total, size, row_total)
    factor = norm_of(projection, square, coeffs, column, gram, row_total)
    norm[...] = jnp.broadcast_to(factor, (1, TILE))
    subtract_basis(new, vector, basis, column)
    new[...] = new[...] / factor


def left_vector(row_total, arrived, image, basis, gram, new, copies, norm):
    total = jnp.sum(arrived[:, 0, :], axis=0, keepdims=True)
    finish(row_total, total, image, basis, gram, new, norm)
    copies[...] = jnp.broadcast_to(new[...].astype(BF16), copies.shape)


def right_vector(row_total, arrived, back, basis, gram, place_row, new, send, norm):
    total = jnp.sum(arrived[:, 0, :], axis=0, keepdims=True)
    finish(row_total, total, back, basis, gram, new, norm)
    hot = one_hot(iota((OWN, NAMED), 0) == place_row[...])
    blocks = dot(hot, new[...].astype(BF16), 0, 0)
    send[...] = blocks.astype(BF16).reshape(send.shape)


def last_vector(row_total, arrived, back, basis, gram, earlier, left_one, left_two, *rest):
    norms, (left_pair, new_pair, factors, new, norm) = rest[:4], rest[4:]
    left_pair[:, 0, :] = left_one[...]
    left_pair[:, 1, :] = left_two[...]
    total = jnp.sum(arrived[:, 0, :], axis=0, keepdims=True)
    finish(row_total, total, back, basis, gram, new, norm)
    new_pair[:, 0, :] = earlier[...]
    new_pair[:, 1, :] = new[...]
    for i, value in enumerate((*norms, norm)):
        factors[i] = jnp.max(value[...])


VMEM = pl.BlockSpec(memory_space=pltpu.VMEM)
HBM = pl.BlockSpec(memory_space=pltpu.HBM)
SMEM = pl.BlockSpec(memory_space=pltpu.SMEM)


def in_hbm(value):
    return pltpu.with_memory_space_constraint(value, pltpu.HBM)


def call(body, outs, args, scratch=(), in_specs=None, out_specs=None, semaphores=0):
    shapes = [jax.ShapeDtypeStruct(s, d) for s, d in outs]
    return pl.pallas_call(
        body,
        out_shape=shapes,
        in_specs=in_specs or [VMEM] * len(args),
        out_specs=out_specs or [VMEM] * len(outs),
        scratch_shapes=[pltpu.VMEM(s, d) for s, d in scratch]
        + [pltpu.SemaphoreType.DMA((semaphores,))] * (semaphores > 0),
        compiler_params=pltpu.CompilerParams(vmem_limit_bytes=8 << 20),
    )(*(in_hbm(a) if spec is HBM else a for a, spec in zip(args, in_specs or args)))


def to_all(value):
    return lax.all_to_all(value, SEND_ALL, 0, 0, tiled=True)


def in_group(value):
    return lax.all_to_all(value, SEND_COL, 0, 0, tiled=True)


def shards(tiles, row_tiles, col_tiles, counts, right_basis, left_basis, start):
    row_total = float(start.shape[0] * DEV)
    with_total = lambda body: functools.partial(body, row_total)
    own = ((OWN, TILE), F32)
    line = ((1, TILE), F32)
    square = ((DEV, TILE), F32)
    sums = ((DEV, 1, TILE), F32)
    blocks = (DEV, PEER_TILES, TILE)
    in_rows = ((8, OWN, TILE), F32)
    copied = ((8, OWN, TILE), BF16)
    work = [((SLOTS, TILE), BF16), ((SLOTS, TILE), F32)]
    right, left = right_basis, left_basis
    begin = start.reshape(OWN, TILE)
    col_row, row_row = col_tiles.reshape(1, SLOTS), row_tiles.reshape(1, SLOTS)

    indices = [((1, SLOTS), I32), ((SLOTS, 1), I32)]
    pay, all_row, all_col, row_row, row_col, begin, right = call(
        first_sums,
        [sums, *indices, *indices, own, (right.shape, F32)],
        (col_row, row_row, right, begin),
        [square, square, indices[0], indices[0]],
        in_specs=[HBM] * 4,
        semaphores=3 + PARTS,
    )
    arrived = to_all(pay)
    pos_row, pos_col, gram_r, gram_l = call(
        tables,
        [*indices, square, square],
        (counts.reshape(1, 1), all_row, all_col, right, left),
        [(left.shape, F32)],
        in_specs=[VMEM] * 4 + [HBM],
        semaphores=1,
    )
    rest, send, place_row = call(
        with_total(first_vector),
        [own, ((DEV, EXTRA, 1, TILE), F32), ((1, NAMED), I32)],
        (arrived, begin, right, gram_r, gram_l, tiles),
        in_specs=[VMEM] * 5 + [HBM],
    )
    partial, beta_zero, gram_row, turned = call(
        with_total(rows_product_first),
        [in_rows, line, line, (tiles.shape, BF16)],
        (to_all(send).reshape(DEV * EXTRA, TILE), pos_col, row_row, tiles),
        work,
    )
    image, pay = call(
        image_sums_first,
        [own, ((DEV, 1, 2 * TILE), F32)],
        (in_group(partial), left, gram_row),
        [square],
    )
    left_one, copies, alpha_one, gram_r, gram_l = call(
        with_total(left_vector_first),
        [own, copied, line, square, square],
        (to_all(pay), image, left),
    )
    (outgoing,) = call(
        column_product, [(blocks, F32)], (in_group(copies), row_col, pos_row, tiles), work
    )
    back, pay = call(
        functools.partial(back_sums, True),
        [own, sums],
        (to_all(outgoing), right, place_row, rest, beta_zero, alpha_one),
        [square],
    )
    right_two, send, beta_one = call(
        with_total(right_vector),
        [own, (blocks, BF16), line],
        (to_all(pay), back, right, gram_r, place_row),
    )
    (partial,) = call(rows_product, [in_rows], (to_all(send), pos_col, row_row, turned), work)
    image, pay = call(
        image_sums, [own, sums], (in_group(partial), left, left_one, beta_one), [square]
    )
    left_two, copies, alpha_two = call(
        with_total(left_vector), [own, copied, line], (to_all(pay), image, left, gram_l)
    )
    (outgoing,) = call(
        column_product, [(blocks, F32)], (in_group(copies), row_col, pos_row, tiles), work
    )
    back, pay = call(
        functools.partial(back_sums, False),
        [own, sums],
        (to_all(outgoing), right, place_row, right_two, beta_one, alpha_two),
        [square],
    )
    norms = (beta_zero, alpha_one, beta_one, alpha_two)
    lefts, rights, factors = call(
        with_total(last_vector),
        [((OWN, 2, TILE), F32)] * 2 + [((5,), F32)],
        (to_all(pay), back, right, gram_r, right_two, left_one, left_two, *norms),
        [own, line],
        out_specs=[VMEM, VMEM, SMEM],
    )
    as_rows = lambda pair: pair.transpose(1, 0, 2).reshape(2, OWN * TILE)
    return as_rows(lefts), as_rows(rights), factors


def solution(mesh):
    torus = Mesh(mesh.devices.reshape(4, 4, 4, 2), ALL)
    placed = (
        P(ALL, None, None),
        P(ALL),
        P(ALL),
        P(ALL),
        P(None, ALL),
        P(None, ALL),
        P(ALL),
    )
    return jax.shard_map(
        shards,
        mesh=torus,
        in_specs=placed,
        out_specs=(P(None, ALL), P(None, ALL), P()),
        check_vma=False,
    )
```

```python
import functools

import jax
import jax.numpy as jnp
from jax import lax
from jax.experimental import pallas as pl
from jax.experimental.pallas import tpu as pltpu
from jax.sharding import Mesh
from jax.sharding import PartitionSpec as P

PEER_TILES = 8
ALL = ("row_0", "row_1", "col_0", "col_1")
SEND_ALL = ("col_1", "col_0", "row_1", "row_0")
SEND_COL = ("col_1", "col_0")
HIGH = lax.Precision.HIGHEST
F32, BF16, I32 = jnp.float32, jnp.bfloat16, jnp.int32

DEV = 128
OWN = 32
TILE = 128
SLOTS = 512
GROUP = 256
NAMED = DEV * PEER_TILES
PLACE = 104
PARTS = 4
SQUARE, DIAGONAL = 126, 127
EXTRA = PEER_TILES + 1


def iota(shape, dim):
    return lax.broadcasted_iota(I32, shape, dim)


def block_of(device):
    near = (device % 2) * 64 + (device // 2 % 4) * 16
    return near + (device // 8 % 4) * 4 + device // 32


def group_row_of(row):
    owner = row // OWN
    return ((owner % 2) * 4 + owner // 2) * OWN + row % OWN


def one_hot(condition):
    return jnp.where(condition, 1.0, 0.0).astype(BF16)


def dot(a, b, ca=1, cb=0, precision=None):
    return lax.dot_general(
        a, b, (((ca,), (cb,)), ((), ())), precision=precision, preferred_element_type=F32
    )


def selected(hot, value):
    first = value.astype(BF16)
    rest = value - first.astype(F32)
    second = rest.astype(BF16)
    third = (rest - second.astype(F32)).astype(BF16)
    return dot(hot, third) + dot(hot, second) + dot(hot, first)


def products_row(basis, vector, held, copies=()):
    size = basis.shape[0]
    total = jnp.zeros((size, TILE), F32)
    for k in range(OWN):
        if copies and k % (OWN // PARTS) == 0:
            copies[k // (OWN // PARTS)].wait()
        total = total + basis[:, k * TILE : (k + 1) * TILE] * vector[k : k + 1, :]
    held[...] = jnp.zeros_like(held)
    held[0:size, :] = total
    row = jnp.sum(held[...].T, axis=0, keepdims=True)
    square = jnp.sum(vector * vector, keepdims=True)
    return jnp.where(iota((1, TILE), 1) == size, square, row)


def coefficients_of(total, size, row_total):
    lane = iota((1, TILE), 1)
    projection = jnp.where(lane < size, total, 0.0)
    square = jnp.sum(jnp.where(lane == size, total, 0.0), axis=1, keepdims=True)
    coeffs = projection / row_total
    diagonal = iota((size, TILE), 0) == iota((size, TILE), 1)
    column = jnp.sum(jnp.where(diagonal, coeffs, 0.0), axis=1, keepdims=True)
    return projection, square, coeffs, column


def subtract_basis(out, vector, basis, column):
    wide = jnp.broadcast_to(column, (column.shape[0], TILE))
    for k in range(OWN):
        part = jnp.sum(basis[:, k * TILE : (k + 1) * TILE] * wide, axis=0, keepdims=True)
        out[k : k + 1, :] = vector[k : k + 1, :] - part


def norm_of(projection, square, coeffs, column, gram, row_total):
    size = column.shape[0]
    applied = jnp.sum(gram[0:size, :] * coeffs, axis=1, keepdims=True)
    quadratic = jnp.sum(applied * column, axis=0, keepdims=True)
    linear = jnp.sum(coeffs * projection, axis=1, keepdims=True)
    left = jnp.maximum(square - 2.0 * linear + quadratic, 0.0)
    return jnp.sqrt(left / row_total + 1e-06)


def first_sums(col_hbm, row_hbm, basis_hbm, start_hbm, out, pos_row, pos_col, row_row, *refs):
    row_col, start, basis, held, listed, col_row, given_row, sems = refs
    wide = basis.shape[1] // PARTS
    parts = [pl.ds(i * wide, wide) for i in range(PARTS)]
    copies = [
        pltpu.make_async_copy(col_hbm, col_row, sems.at[0]),
        pltpu.make_async_copy(row_hbm, given_row, sems.at[1]),
        pltpu.make_async_copy(start_hbm, start, sems.at[2]),
    ]
    copies += [
        pltpu.make_async_copy(basis_hbm.at[:, part], basis.at[:, part], sems.at[3 + i])
        for i, part in enumerate(parts)
    ]
    for copy in copies:
        copy.start()
    copies[0].wait()
    owner, place = block_of(col_row[...] // OWN), col_row[...] % OWN
    owners = one_hot(iota((DEV, SLOTS), 0) == owner)
    in_place = iota((OWN, SLOTS), 0) == place
    touched = dot(one_hot(in_place), owners, 1, 1) > 0.5
    below = one_hot(iota((OWN, OWN), 1) < iota((OWN, OWN), 0))
    rank = dot(below, one_hot(touched))
    listed[...] = jnp.zeros_like(listed)
    number = (iota((OWN, DEV), 0) + 1).astype(F32)
    for k in range(PEER_TILES):
        here = touched & (rank > k - 0.5) & (rank < k + 0.5)
        named = jnp.sum(jnp.where(here, number, 0.0), axis=0, keepdims=True)
        listed[PLACE + k : PLACE + k + 1, :] = named - 1.0
    places = listed[...].T
    mine = jnp.where(in_place, dot(rank.astype(BF16), owners), 0.0)
    position = owner * PEER_TILES + jnp.sum(mine, axis=0, keepdims=True).astype(I32)
    pos_row[...] = position
    copies[1].wait()
    row = group_row_of(given_row[...])
    row_row[...] = row
    both = jnp.where(iota((8, SLOTS), 0) == 0, position, row)
    columns = both.astype(F32).T.astype(I32)
    pos_col[...] = columns[:, 0:1]
    row_col[...] = columns[:, 1:2]
    copies[2].wait()
    out[:, 0, :] = places + products_row(basis, start[...], held, copies[3:])


def gram_of(basis):
    value = basis[...]
    first = value.astype(BF16)
    rest = value - first.astype(F32)
    second = rest.astype(BF16)
    third = (rest - second.astype(F32)).astype(BF16)
    low = dot(third, first, 1, 1)
    middle = dot(second, first, 1, 1)
    both = low + middle
    return dot(second, second, 1, 1) + (both + both.T) + dot(first, first, 1, 1)


def tables(counts, all_row, all_col, right, left_hbm, pos_row, pos_col, gram_r, gram_l, left, sems):
    copy = pltpu.make_async_copy(left_hbm, left, sems.at[0])
    copy.start()
    size = right.shape[0]
    gram_r[...] = jnp.zeros_like(gram_r)
    gram_l[...] = jnp.zeros_like(gram_l)
    gram_r[0:size, 0:size] = gram_of(right)
    copy.wait()
    gram_l[0:size, 0:size] = gram_of(left)
    pos_row[...] = jnp.where(iota((1, SLOTS), 1) < counts[...], all_row[...], -1)
    pos_col[...] = jnp.where(iota((SLOTS, 1), 0) < counts[...], all_col[...], -1)


def place_row_of(arrived):
    lane = iota((DEV, NAMED), 0)
    spread = dot(arrived.astype(BF16), one_hot(lane - PLACE == iota((DEV, NAMED), 1) % PEER_TILES))
    own = iota((DEV, NAMED), 1) // PEER_TILES == lane
    row = jnp.sum(jnp.where(own, spread, 0.0), axis=0, keepdims=True)
    return jnp.round(row).astype(I32)


def first_vector(row_total, arrived, start, basis, gram_r, gram_l, _, rest, send, place_row):
    size = basis.shape[0]
    got = arrived[:, 0, :]
    total = jnp.sum(got, axis=0, keepdims=True)
    _, _, _, column = coefficients_of(total, size, row_total)
    named = place_row_of(got)
    place_row[...] = named
    subtract_basis(rest, start, basis, column)
    vector = rest[...]
    hot = jnp.where(iota((OWN, NAMED), 0) == named, 1.0, 0.0)
    blocks = dot(hot, vector, 0, 0, HIGH).reshape(DEV, PEER_TILES, TILE)
    for k in range(PEER_TILES):
        send[:, k, 0, :] = blocks[:, k, :]
    square = jnp.sum(vector * vector, keepdims=True)
    row, lane = iota((DEV, TILE), 0), iota((DEV, TILE), 1)
    diagonal = jnp.sum(jnp.where(row == lane, gram_r[...], 0.0), axis=1, keepdims=True)
    packed = jnp.where(row > lane, gram_r[...], gram_l[...])
    packed = jnp.where(lane == DIAGONAL, diagonal, packed)
    send[:, PEER_TILES, 0, :] = jnp.where(lane == SQUARE, square, packed)


def tiles_times(sources, tiles, products):
    many = 16
    row = iota((many, TILE), 0)

    for at in range(0, SLOTS, many):
        block = tiles[pl.ds(at, many)].reshape(many * TILE, TILE)
        wide = dot(sources[pl.ds(at, many), :], block, 1, 1)
        total = wide[:, 0:TILE]
        for j in range(1, many):
            total = jnp.where(row == j, wide[:, j * TILE : (j + 1) * TILE], total)
        products[pl.ds(at, many), :] = total


def tiles_times_turned(sources, tiles, products, turned):
    many = 16
    row = iota((many, TILE), 0)
    for at in range(0, SLOTS, many):
        mine = sources[pl.ds(at, many), :]
        blocks = [tiles[at + j].T for j in range(many)]
        for j in range(many):
            turned[at + j] = blocks[j]
        parts = [jnp.where(row == j, mine, jnp.zeros_like(mine)) for j in range(many)]
        block = jnp.concatenate(blocks, axis=0)
        products[pl.ds(at, many), :] = dot(jnp.concatenate(parts, axis=1), block)


def times_tiles(sources, tiles, products):
    many = 16
    row = iota((many, TILE), 0)

    def step(i, carry):
        at = pl.multiple_of(i * many, many)
        block = tiles[pl.ds(at, many)].reshape(many * TILE, TILE)
        mine = sources[pl.ds(at, many), :]
        parts = [jnp.where(row == j, mine, jnp.zeros_like(mine)) for j in range(many)]
        products[pl.ds(at, many), :] = dot(jnp.concatenate(parts, axis=1), block)
        return carry

    lax.fori_loop(0, SLOTS // many, step, 0, unroll=True)


def summed_by_row(row_row, products, out):
    rows = one_hot(iota((GROUP, SLOTS), 0) == row_row[...])
    out[...] = selected(rows, products[...]).reshape(out.shape)


def rows_product_first(
    row_total, arrived, pos_col, row_row, tiles, out, norm, gram_row, turned, sources, products
):
    part = lambda k: arrived[pl.ds(k, DEV, stride=EXTRA), :]
    total = jnp.sum(part(PEER_TILES), axis=0, keepdims=True)
    gram_row[...] = total
    total = jnp.sum(jnp.where(iota((1, TILE), 1) == SQUARE, total, 0.0), axis=1, keepdims=True)
    size = jnp.sqrt(total / row_total + 1e-06)
    norm[...] = jnp.broadcast_to(size, (1, TILE))
    values = jnp.zeros((SLOTS, TILE), F32)
    position = pos_col[...]
    for k in range(PEER_TILES):
        vector = (part(k) / size).astype(BF16)
        hot = one_hot(iota((SLOTS, DEV), 1) * PEER_TILES + k == position)
        values = values + dot(hot, vector)
    sources[...] = values.astype(BF16)
    tiles_times_turned(sources, tiles, products, turned)
    summed_by_row(row_row, products, out)


def rows_product(arrived, pos_col, row_row, tiles, out, sources, products):
    hot = one_hot(iota((SLOTS, NAMED), 1) == pos_col[...])
    vector = arrived[...].reshape(NAMED, TILE)
    sources[...] = dot(hot, vector).astype(BF16)
    times_tiles(sources, tiles, products)
    summed_by_row(row_row, products, out)


def column_product(arrived, row_col, pos_row, tiles, out, sources, products):
    hot = one_hot(iota((SLOTS, GROUP), 1) == row_col[...])
    vector = arrived[...].reshape(GROUP, TILE)
    sources[...] = dot(hot, vector).astype(BF16)
    times_tiles(sources, tiles, products)
    hot = one_hot(iota((NAMED, SLOTS), 0) == pos_row[...])
    out[...] = selected(hot, products[...]).reshape(out.shape)


def image_sums_first(arrived, basis, gram_row, image, out, held):
    vector = jnp.sum(arrived[...], axis=0)
    image[...] = vector
    row = products_row(basis, vector, held)
    out[:, 0, 0:TILE] = jnp.broadcast_to(row, (DEV, TILE))
    out[:, 0, TILE : 2 * TILE] = jnp.broadcast_to(gram_row[...], (DEV, TILE))


def image_sums(arrived, basis, earlier, factor, image, out, held):
    vector = jnp.sum(arrived[...], axis=0) - factor[...] * earlier[...]
    image[...] = vector
    out[:, 0, :] = jnp.broadcast_to(products_row(basis, vector, held), (DEV, TILE))


def back_sums(divide, arrived, basis, place_row, earlier, by, factor, back, out, held):
    hot = one_hot(iota((OWN, NAMED), 0) == place_row[...])
    before = earlier[...] / by[...] if divide else earlier[...]
    vector = selected(hot, arrived[...].reshape(NAMED, TILE)) - factor[...] * before
    back[...] = vector
    out[:, 0, :] = jnp.broadcast_to(products_row(basis, vector, held), (DEV, TILE))


def left_vector_first(row_total, arrived, image, basis, new, copies, norm, gram_r, gram_l):
    got = arrived[:, 0, :]
    both = got[:, TILE : 2 * TILE]
    row, lane = iota((DEV, TILE), 0), iota((DEV, TILE), 1)
    diagonal = jnp.sum(jnp.where(lane == DIAGONAL, both, 0.0), axis=1, keepdims=True)
    gram_r[...] = jnp.where(row > lane, both + both, jnp.where(row == lane, diagonal, 0.0))
    upper = jnp.where(row < lane, both + both, jnp.where(row == lane, both, 0.0))
    gram_l[...] = jnp.where(lane < basis.shape[0], upper, 0.0)
    total = jnp.sum(got[:, 0:TILE], axis=0, keepdims=True)
    finish(row_total, total, image, basis, gram_l, new, norm)
    copies[...] = jnp.broadcast_to(new[...].astype(BF16), copies.shape)


def finish(row_total, total, vector, basis, gram, new, norm):
    size = basis.shape[0]
    projection, square, coeffs, column = coefficients_of(total, size, row_total)
    factor = norm_of(projection, square, coeffs, column, gram, row_total)
    norm[...] = jnp.broadcast_to(factor, (1, TILE))
    subtract_basis(new, vector, basis, column)
    new[...] = new[...] / factor


def left_vector(row_total, arrived, image, basis, gram, new, copies, norm):
    total = jnp.sum(arrived[:, 0, :], axis=0, keepdims=True)
    finish(row_total, total, image, basis, gram, new, norm)
    copies[...] = jnp.broadcast_to(new[...].astype(BF16), copies.shape)


def right_vector(row_total, arrived, back, basis, gram, place_row, new, send, norm):
    total = jnp.sum(arrived[:, 0, :], axis=0, keepdims=True)
    finish(row_total, total, back, basis, gram, new, norm)
    hot = one_hot(iota((OWN, NAMED), 0) == place_row[...])
    blocks = dot(hot, new[...].astype(BF16), 0, 0)
    send[...] = blocks.astype(BF16).reshape(send.shape)


def last_vector(row_total, arrived, back, basis, gram, earlier, left_one, left_two, *rest):
    norms, (left_pair, new_pair, factors, new, norm) = rest[:4], rest[4:]
    for i, value in enumerate(norms):
        factors[i] = value[0, 0]
    left_pair[:, 0, :] = left_one[...]
    left_pair[:, 1, :] = left_two[...]
    total = jnp.sum(arrived[:, 0, :], axis=0, keepdims=True)
    finish(row_total, total, back, basis, gram, new, norm)
    new_pair[:, 0, :] = earlier[...]
    new_pair[:, 1, :] = new[...]
    factors[len(norms)] = norm[0, 0]


VMEM = pl.BlockSpec(memory_space=pltpu.VMEM)
HBM = pl.BlockSpec(memory_space=pltpu.HBM)
SMEM = pl.BlockSpec(memory_space=pltpu.SMEM)


def in_hbm(value):
    return pltpu.with_memory_space_constraint(value, pltpu.HBM)


def call(body, outs, args, scratch=(), in_specs=None, out_specs=None, semaphores=0):
    shapes = [jax.ShapeDtypeStruct(s, d) for s, d in outs]
    return pl.pallas_call(
        body,
        out_shape=shapes,
        in_specs=in_specs or [VMEM] * len(args),
        out_specs=out_specs or [VMEM] * len(outs),
        scratch_shapes=[pltpu.VMEM(s, d) for s, d in scratch]
        + [pltpu.SemaphoreType.DMA((semaphores,))] * (semaphores > 0),
        compiler_params=pltpu.CompilerParams(vmem_limit_bytes=8 << 20),
    )(*(in_hbm(a) if spec is HBM else a for a, spec in zip(args, in_specs or args)))


def to_all(value):
    return lax.all_to_all(value, SEND_ALL, 0, 0, tiled=True)


def in_group(value):
    return lax.all_to_all(value, SEND_COL, 0, 0, tiled=True)


def shards(tiles, row_tiles, col_tiles, counts, right_basis, left_basis, start):
    row_total = float(start.shape[0] * DEV)
    with_total = lambda body: functools.partial(body, row_total)
    own = ((OWN, TILE), F32)
    line = ((1, TILE), F32)
    square = ((DEV, TILE), F32)
    sums = ((DEV, 1, TILE), F32)
    blocks = (DEV, PEER_TILES, TILE)
    in_rows = ((8, OWN, TILE), F32)
    copied = ((8, OWN, TILE), BF16)
    work = [((SLOTS, TILE), BF16), ((SLOTS, TILE), F32)]
    right, left = right_basis, left_basis
    begin = start.reshape(OWN, TILE)
    col_row, row_row = col_tiles.reshape(1, SLOTS), row_tiles.reshape(1, SLOTS)

    indices = [((1, SLOTS), I32), ((SLOTS, 1), I32)]
    pay, all_row, all_col, row_row, row_col, begin, right = call(
        first_sums,
        [sums, *indices, *indices, own, (right.shape, F32)],
        (col_row, row_row, right, begin),
        [square, square, indices[0], indices[0]],
        in_specs=[HBM] * 4,
        semaphores=3 + PARTS,
    )
    arrived = to_all(pay)
    pos_row, pos_col, gram_r, gram_l = call(
        tables,
        [*indices, square, square],
        (counts.reshape(1, 1), all_row, all_col, right, left),
        [(left.shape, F32)],
        in_specs=[VMEM] * 4 + [HBM],
        semaphores=1,
    )
    rest, send, place_row = call(
        with_total(first_vector),
        [own, ((DEV, EXTRA, 1, TILE), F32), ((1, NAMED), I32)],
        (arrived, begin, right, gram_r, gram_l, tiles),
        in_specs=[VMEM] * 5 + [HBM],
    )
    partial, beta_zero, gram_row, turned = call(
        with_total(rows_product_first),
        [in_rows, line, line, (tiles.shape, BF16)],
        (to_all(send).reshape(DEV * EXTRA, TILE), pos_col, row_row, tiles),
        work,
    )
    image, pay = call(
        image_sums_first,
        [own, ((DEV, 1, 2 * TILE), F32)],
        (in_group(partial), left, gram_row),
        [square],
    )
    left_one, copies, alpha_one, gram_r, gram_l = call(
        with_total(left_vector_first),
        [own, copied, line, square, square],
        (to_all(pay), image, left),
    )
    (outgoing,) = call(
        column_product, [(blocks, F32)], (in_group(copies), row_col, pos_row, tiles), work
    )
    back, pay = call(
        functools.partial(back_sums, True),
        [own, sums],
        (to_all(outgoing), right, place_row, rest, beta_zero, alpha_one),
        [square],
    )
    right_two, send, beta_one = call(
        with_total(right_vector),
        [own, (blocks, BF16), line],
        (to_all(pay), back, right, gram_r, place_row),
    )
    (partial,) = call(rows_product, [in_rows], (to_all(send), pos_col, row_row, turned), work)
    image, pay = call(
        image_sums, [own, sums], (in_group(partial), left, left_one, beta_one), [square]
    )
    left_two, copies, alpha_two = call(
        with_total(left_vector), [own, copied, line], (to_all(pay), image, left, gram_l)
    )
    (outgoing,) = call(
        column_product, [(blocks, F32)], (in_group(copies), row_col, pos_row, tiles), work
    )
    back, pay = call(
        functools.partial(back_sums, False),
        [own, sums],
        (to_all(outgoing), right, place_row, right_two, beta_one, alpha_two),
        [square],
    )
    norms = (beta_zero, alpha_one, beta_one, alpha_two)
    lefts, rights, factors = call(
        with_total(last_vector),
        [((OWN, 2, TILE), F32)] * 2 + [((5,), F32)],
        (to_all(pay), back, right, gram_r, right_two, left_one, left_two, *norms),
        [own, line],
        out_specs=[VMEM, VMEM, SMEM],
    )
    as_rows = lambda pair: pair.transpose(1, 0, 2).reshape(2, OWN * TILE)
    return as_rows(lefts), as_rows(rights), factors


def solution(mesh):
    torus = Mesh(mesh.devices.reshape(4, 4, 4, 2), ALL)
    placed = (
        P(ALL, None, None),
        P(ALL),
        P(ALL),
        P(ALL),
        P(None, ALL),
        P(None, ALL),
        P(ALL),
    )
    return jax.shard_map(
        shards,
        mesh=torus,
        in_specs=placed,
        out_specs=(P(None, ALL), P(None, ALL), P()),
        check_vma=False,
    )
```
